512 devices in a mesh: seq: 32 (over x, z), exp: 16 (over y, core).
Axes of the slice: x: 4, y: 8, z: 8, core: 2. Of those that a mesh axis runs over, the one named last changes fastest.
Arguments:
- query_tok: bfloat16 [32768, 4096], P('seq', 'exp'), may hold values from -6 to 6
- key_tok: bfloat16 [32768, 4096], P('seq', 'exp'), may hold values from -6 to 6
- value_tok: bfloat16 [32768, 4096], P('seq', 'exp'), may hold values from -6 to 6
- grad_out: bfloat16 [32768, 4096], P('seq', 'exp'), may hold values from -6 to 6
- decay_rate: float32 [32], P('exp'), may hold values from 1.8626451e-07 to 0.025
Outputs:
- attended: bfloat16 [32768, 4096], P(('seq', 'exp'))
- query_gradient: bfloat16 [32768, 4096], P(('seq', 'exp'))
- key_gradient: bfloat16 [32768, 4096], P(('seq', 'exp'))
- value_gradient: bfloat16 [32768, 4096], P(('seq', 'exp'))
The draws below stay inside these ranges and needn't reach their ends.
All inputs are finite; a program needn't handle non-finite values.
Results may differ from the reference program's by a relative error of at most 0.0048.
Values may be sent and summed in bfloat16 or wider, within the bound.
A program may use at most 64 MiB of HBM per device.

```python
import math
import jax
import jax.numpy as jnp
from jax import lax

H = 32
HEAD = 128
TOKENS = 32768
BLK = 1024


def block_levels(own_key, dims, cuts, smallest, top_value):
    level, own = 1.0, jax.random.fold_in(own_key, 6)
    for dim, shards_of in cuts:
        steps = jnp.exp(jax.random.uniform(jax.random.fold_in(own, dim), (shards_of,), jnp.float32, smallest / len(cuts), top_value / len(cuts)))
        level = level * jnp.repeat(steps, dims[dim] // shards_of).reshape([-1 if axis == dim else 1 for axis in range(len(dims))])
    return level


def centred(own_key, shape, width, most, pieces=(), kind=jnp.bfloat16):
    drawn = width * jax.random.normal(own_key, shape, jnp.float32)
    if pieces:
        drawn = drawn * block_levels(own_key, shape, pieces, -0.22, 0.18)
    return jnp.clip(drawn, -most, most).astype(kind)


def setup_inputs(seed: int = 0) -> dict:
    arg_keys = jax.random.split(jax.random.key(seed), 6)
    query_tok = centred(arg_keys[0], (TOKENS, H * HEAD), 1.0, 6.0, ((0, 32), (1, 16)))
    key_tok = centred(arg_keys[1], (TOKENS, H * HEAD), 1.0, 6.0, ((0, 32), (1, 16)))
    value_tok = centred(arg_keys[2], (TOKENS, H * HEAD), 1.0, 6.0, ((0, 32), (1, 16)))
    grad_out = centred(arg_keys[3], (TOKENS, H * HEAD), 1.0, 6.0, ((0, 32), (1, 16)))
    decay_rate = jnp.clip(jnp.exp(math.log(0.025) - 11.807219 * jax.random.uniform(arg_keys[4], (H,), jnp.float32) ** block_levels(arg_keys[4], (H,), ((0, 16),), -0.2, 0.2)), 1.862645149230957e-07, 0.025)
    return {"query_tok": query_tok, "key_tok": key_tok, "value_tok": value_tok, "grad_out": grad_out, "decay_rate": decay_rate}


def head_pass(inputs):
    query_head, key_head, value_head, upstream_head, rate_head = inputs
    greatest_precision = lax.Precision.HIGHEST
    position = jnp.arange(BLK, dtype=jnp.float32)
    scale_head = jnp.sqrt((2.0 * rate_head + 2.0 / TOKENS) / HEAD)
    to_end = jnp.exp(-rate_head * (BLK - position))[None, :, None]
    from_start = jnp.exp(-rate_head * (position + 1.0))[None, :, None]
    key_product = (key_head.astype(jnp.float32) * to_end).astype(jnp.bfloat16)
    query_product = (query_head.astype(jnp.float32) * from_start).astype(jnp.bfloat16)
    query_broad = query_head.astype(jnp.float32)
    key_broad = key_head.astype(jnp.float32)
    value_broad = value_head.astype(jnp.float32)
    upstream_broad = upstream_head.astype(jnp.float32)
    state_from_keys = jnp.einsum('ypv,ypf->yvf', key_product.astype(jnp.float32), value_broad, precision=greatest_precision)
    state_from_queries = jnp.einsum('ypv,ypf->yvf', query_product.astype(jnp.float32), upstream_broad, precision=greatest_precision)
    step_decay = jnp.exp(-rate_head * BLK)

    def decay_step(state, latest):
        return (step_decay * state + latest, state)
    zero_state = jnp.zeros((HEAD, HEAD), jnp.float32)
    _, initial_state_list = lax.scan(decay_step, zero_state, state_from_keys)
    _, final_state_list = lax.scan(decay_step, zero_state, state_from_queries, reverse=True)
    offsets = position[:, None] - position[None, :]
    damping = jnp.where(offsets >= 0, jnp.exp(-rate_head * jnp.maximum(offsets, 0.0)), 0.0) * scale_head
    scores = jnp.einsum('nid,njd->nij', query_broad, key_broad, precision=greatest_precision)
    weights = (scores * damping[None]).astype(jnp.bfloat16).astype(jnp.float32)
    grad_scores = jnp.einsum('nid,njd->nij', upstream_broad, value_broad, precision=greatest_precision)
    gweights = (grad_scores * damping[None]).astype(jnp.bfloat16).astype(jnp.float32)
    leading_scale = (scale_head * jnp.exp(-rate_head * position))[None, :, None]
    trailing_scale = (scale_head * jnp.exp(-rate_head * (BLK - 1.0 - position)))[None, :, None]
    attended = jnp.einsum('nij,njd->nid', weights, value_broad, precision=greatest_precision)
    attended = attended + leading_scale * jnp.einsum('vkx,vxg->vkg', query_broad, initial_state_list, precision=greatest_precision)
    query_gradient = jnp.einsum('nij,njd->nid', gweights, key_broad, precision=greatest_precision)
    query_gradient = query_gradient + leading_scale * jnp.einsum('rwp,rmp->rwm', upstream_broad, initial_state_list, precision=greatest_precision)
    key_gradient = jnp.einsum('nij,nid->njd', gweights, query_broad, precision=greatest_precision)
    key_gradient = key_gradient + trailing_scale * jnp.einsum('rwp,rmp->rwm', value_broad, final_state_list, precision=greatest_precision)
    value_gradient = jnp.einsum('nij,nid->njd', weights, upstream_broad, precision=greatest_precision)
    value_gradient = value_gradient + trailing_scale * jnp.einsum('vkx,vxg->vkg', key_broad, final_state_list, precision=greatest_precision)
    return (attended.astype(jnp.bfloat16), query_gradient.astype(jnp.bfloat16), key_gradient.astype(jnp.bfloat16), value_gradient.astype(jnp.bfloat16))

def split_heads(whole):
    return whole.reshape(TOKENS // BLK, BLK, H, HEAD).transpose(2, 0, 1, 3)

def join_heads(parted):
    return parted.transpose(1, 2, 0, 3).reshape(TOKENS, H * HEAD)

def reference(query_tok, key_tok, value_tok, grad_out, decay_rate):
    results = lax.map(head_pass, (split_heads(query_tok), split_heads(key_tok), split_heads(value_tok), split_heads(grad_out), decay_rate.astype(jnp.float32)))
    return (join_heads(results[0]), join_heads(results[1]), join_heads(results[2]), join_heads(results[3]))
```

```python
import jax
import jax.numpy as jnp
from jax import lax
from jax.sharding import PartitionSpec as P


def decayed_scan(part, rate_len, axis, reverse):
    count = lax.axis_size(axis)
    place = lax.axis_index(axis)
    ahead = count - 1 - place if reverse else place
    sign = -1 if reverse else 1

    def shifted(x, d):
        pairs = [(s, s + sign * d) for s in range(count) if 0 <= s + sign * d < count]
        return lax.ppermute(x, axis, pairs)

    def weight(d):
        return jnp.exp(-rate_len * d)[:, None, None]

    total = part
    d = 1
    while 2 * d < count:
        got = shifted(total, d)
        total = total + jnp.where(ahead >= d, weight(d), 0.0) * got
        d *= 2
    near = shifted(total, 1)
    far_d = d + 1
    result = jnp.where(ahead >= 1, 1.0, 0.0) * near
    if far_d < count:
        far = shifted(total, far_d)
        result = result + jnp.where(ahead >= far_d, weight(d), 0.0) * far
    return result


def shards(query_tok, key_tok, value_tok, grad_out, decay_rate):
    greatest_precision = lax.Precision.HIGHEST
    seg_len = query_tok.shape[0]
    num_heads = decay_rate.shape[0]
    head_size = query_tok.shape[1] // num_heads
    total_len = seg_len * lax.axis_size("seq")
    scale_head = jnp.sqrt((2.0 * decay_rate + 2.0 / total_len) / head_size)
    shape_three = (seg_len, num_heads, head_size)
    query_heads = query_tok.reshape(shape_three)
    key_heads = key_tok.reshape(shape_three)
    value_heads = value_tok.reshape(shape_three)
    upstream = grad_out.reshape(shape_three)
    position = jnp.arange(seg_len, dtype=jnp.float32)
    to_end = jnp.exp(-decay_rate[None, :] * (seg_len - position[:, None]))
    from_start = jnp.exp(-decay_rate[None, :] * (position[:, None] + 1.0))
    key_product = (key_heads * to_end[:, :, None]).astype(jnp.bfloat16)
    query_product = (query_heads * from_start[:, :, None]).astype(jnp.bfloat16)
    dev_key = jnp.einsum(
        "ihd,ihe->hde", key_product, value_heads, preferred_element_type=jnp.float32
    )
    dev_query = jnp.einsum(
        "ihd,ihe->hde", query_product, upstream, preferred_element_type=jnp.float32
    )
    rate_len = decay_rate * seg_len
    incoming = decayed_scan(dev_key, rate_len, "seq", False)
    outgoing = decayed_scan(dev_query, rate_len, "seq", True)
    offsets = position[:, None] - position[None, :]
    over_rows = (((0,), (0,)), ((), ()))
    over_cols = (((1,), (1,)), ((), ()))

    def head_work(index):
        rate = decay_rate[index]
        scale = scale_head[index]
        query_one = query_heads[:, index, :]
        key_one = key_heads[:, index, :]
        value_one = value_heads[:, index, :]
        upstream_one = upstream[:, index, :]
        start_state = incoming[index]
        end_state = outgoing[index]
        damping = jnp.where(offsets >= 0, jnp.exp(-rate * jnp.maximum(offsets, 0.0)), 0.0) * scale
        scores = lax.dot_general(query_one, key_one, over_cols, preferred_element_type=jnp.float32)
        weights = (scores * damping).astype(jnp.bfloat16)
        grad_scores = lax.dot_general(
            upstream_one, value_one, over_cols, preferred_element_type=jnp.float32
        )
        gweights = (grad_scores * damping).astype(jnp.bfloat16)
        leading_scale = (scale * jnp.exp(-rate * position))[:, None]
        trailing_scale = (scale * jnp.exp(-rate * (seg_len - 1.0 - position)))[:, None]
        attended = jnp.dot(weights, value_one, preferred_element_type=jnp.float32)
        attended = attended + leading_scale * jnp.dot(
            query_one.astype(jnp.float32), start_state, precision=greatest_precision
        )
        query_gradient = jnp.dot(gweights, key_one, preferred_element_type=jnp.float32)
        query_gradient = query_gradient + leading_scale * lax.dot_general(
            upstream_one.astype(jnp.float32), start_state, over_cols, precision=greatest_precision
        )
        key_gradient = lax.dot_general(
            gweights, query_one, over_rows, preferred_element_type=jnp.float32
        )
        key_gradient = key_gradient + trailing_scale * lax.dot_general(
            value_one.astype(jnp.float32), end_state, over_cols, precision=greatest_precision
        )
        value_gradient = lax.dot_general(
            weights, upstream_one, over_rows, preferred_element_type=jnp.float32
        )
        value_gradient = value_gradient + trailing_scale * jnp.dot(
            key_one.astype(jnp.float32), end_state, precision=greatest_precision
        )
        return (
            attended.astype(jnp.bfloat16),
            query_gradient.astype(jnp.bfloat16),
            key_gradient.astype(jnp.bfloat16),
            value_gradient.astype(jnp.bfloat16),
        )

    head_outputs = [head_work(index) for index in range(num_heads)]
    results = tuple(
        (
            jnp.stack([single[member] for single in head_outputs], axis=1).reshape(
                seg_len, num_heads * head_size
            )
            for member in range(4)
        )
    )
    return lax.all_to_all(results, "exp", split_axis=0, concat_axis=1, tiled=True)


def solution(mesh):
    placed = (P("seq", "exp"), P("seq", "exp"), P("seq", "exp"), P("seq", "exp"), P("exp"))
    return jax.shard_map(
        shards,
        mesh=mesh,
        in_specs=placed,
        out_specs=(
            P(("seq", "exp"), None),
            P(("seq", "exp"), None),
            P(("seq", "exp"), None),
            P(("seq", "exp"), None),
        ),
        check_vma=False,
    )
```

```python
import functools

import jax
import jax.numpy as jnp
from jax import lax
from jax.experimental import pallas as pl
from jax.experimental.pallas import tpu as pltpu
from jax.sharding import PartitionSpec as P


MESH = pl.DeviceIdType.MESH


def scan_kernel(n, near, far, w_ref, k_ref, q_ref, s_out, r_out, kx, qx, krecv, qrecv, sems):
    me = lax.axis_index("seq")
    ex = lax.axis_index("exp")
    heads = k_ref.shape[0]
    barrier = pltpu.get_barrier_semaphore()
    partners = sorted(set(near + [1, far]))
    for d in partners:
        for other in (me + d, me - d):
            @pl.when(jnp.logical_and(other >= 0, other < n))
            def _():
                pl.semaphore_signal(barrier, 1, device_id=(other, ex), device_id_type=MESH)
    peers = 0
    for d in partners:
        for other in (me + d, me - d):
            peers = peers + jnp.logical_and(other >= 0, other < n).astype(jnp.int32)
    pl.semaphore_wait(barrier, peers)

    def copy(src, dst, slot, other):
        return pltpu.make_async_remote_copy(
            src_ref=src, dst_ref=dst, send_sem=sems.at[0, slot], recv_sem=sems.at[1, slot],
            device_id=(lax.rem(other + n, n), ex), device_id_type=MESH,
        )

    sent = []
    kcur, qcur = k_ref, q_ref
    for r, d in enumerate(near):
        kc = copy(kcur, krecv.at[r], 2 * r, me + d)
        qc = copy(qcur, qrecv.at[r], 2 * r + 1, me - d)
        pl.when(me + d < n)(kc.start)
        pl.when(me - d >= 0)(qc.start)
        sent.append((kc, me + d < n))
        sent.append((qc, me - d >= 0))
        for cur, nxt, recv, cp, has in ((kcur, kx, krecv, kc, me - d >= 0), (qcur, qx, qrecv, qc, me + d < n)):
            @pl.when(has)
            def _():
                cp.wait_recv()
                for h in range(heads):
                    nxt[r, h] = cur[h] + w_ref[r * heads + h] * recv[r, h]

            @pl.when(jnp.logical_not(has))
            def _():
                nxt[r] = cur[...]
        kcur, qcur = kx.at[r], qx.at[r]
    last = len(near)
    finals = []
    for j, d in enumerate((1, far)):
        slot = 2 * (last + j)
        kc = copy(kcur, krecv.at[last + j], slot, me + d)
        qc = copy(qcur, qrecv.at[last + j], slot + 1, me - d)
        pl.when(me + d < n)(kc.start)
        pl.when(me - d >= 0)(qc.start)
        sent.append((kc, me + d < n))
        sent.append((qc, me - d >= 0))
        finals.append((kc, qc, d))
    s_out[...] = jnp.zeros_like(s_out)
    r_out[...] = jnp.zeros_like(r_out)
    for j, (kc, qc, d) in enumerate(finals):
        for cp, recv, out, has in ((kc, krecv, s_out, me - d >= 0), (qc, qrecv, r_out, me + d < n)):
            @pl.when(has)
            def _():
                cp.wait_recv()
                for h in range(heads):
                    scale = 1.0 if j == 0 else w_ref[last * heads + h]
                    out[h] = out[h] + scale * recv[last + j, h]
    for cp, cond in sent:
        pl.when(cond)(cp.wait_send)


def state_scan(dev_key, dev_query, rate_len, n):
    near = []
    d = 1
    while 2 * d < n:
        near.append(d)
        d *= 2
    far = d + 1
    heads = dev_key.shape[0]
    dists = jnp.asarray(near + [d], jnp.float32)
    weights = jnp.exp(-dists[:, None] * rate_len[None, :]).reshape(-1)
    nrecv = len(near) + 2
    body = functools.partial(scan_kernel, n, near, far)
    state = jax.ShapeDtypeStruct(dev_key.shape, jnp.float32)
    vspec = pl.BlockSpec(memory_space=pltpu.VMEM)
    return pl.pallas_call(
        body,
        out_shape=(state, state),
        in_specs=[pl.BlockSpec(memory_space=pltpu.SMEM), vspec, vspec],
        out_specs=(vspec, vspec),
        scratch_shapes=[
            pltpu.VMEM((len(near),) + dev_key.shape, jnp.float32),
            pltpu.VMEM((len(near),) + dev_key.shape, jnp.float32),
            pltpu.VMEM((nrecv,) + dev_key.shape, jnp.float32),
            pltpu.VMEM((nrecv,) + dev_key.shape, jnp.float32),
            pltpu.SemaphoreType.DMA((2, 2 * nrecv)),
        ],
        compiler_params=pltpu.CompilerParams(collective_id=0, has_side_effects=True),
    )(weights, dev_key, dev_query)


def shards(query_tok, key_tok, value_tok, grad_out, decay_rate):
    greatest_precision = lax.Precision.HIGHEST
    seg_len = query_tok.shape[0]
    num_heads = decay_rate.shape[0]
    head_size = query_tok.shape[1] // num_heads
    total_len = seg_len * lax.axis_size("seq")
    scale_head = jnp.sqrt((2.0 * decay_rate + 2.0 / total_len) / head_size)
    shape_three = (seg_len, num_heads, head_size)
    query_heads = query_tok.reshape(shape_three)
    key_heads = key_tok.reshape(shape_three)
    value_heads = value_tok.reshape(shape_three)
    upstream = grad_out.reshape(shape_three)
    position = jnp.arange(seg_len, dtype=jnp.float32)
    to_end = jnp.exp(-decay_rate[None, :] * (seg_len - position[:, None]))
    from_start = jnp.exp(-decay_rate[None, :] * (position[:, None] + 1.0))
    key_product = (key_heads * to_end[:, :, None]).astype(jnp.bfloat16)
    query_product = (query_heads * from_start[:, :, None]).astype(jnp.bfloat16)
    dev_key = jnp.einsum(
        "ihd,ihe->hde", key_product, value_heads, preferred_element_type=jnp.float32
    )
    dev_query = jnp.einsum(
        "ihd,ihe->hde", query_product, upstream, preferred_element_type=jnp.float32
    )
    rate_len = decay_rate * seg_len
    incoming, outgoing = state_scan(dev_key, dev_query, rate_len, lax.axis_size("seq"))
    offsets = position[:, None] - position[None, :]
    over_rows = (((0,), (0,)), ((), ()))
    over_cols = (((1,), (1,)), ((), ()))

    def head_work(index):
        rate = decay_rate[index]
        scale = scale_head[index]
        query_one = query_heads[:, index, :]
        key_one = key_heads[:, index, :]
        value_one = value_heads[:, index, :]
        upstream_one = upstream[:, index, :]
        start_state = incoming[index]
        end_state = outgoing[index]
        damping = jnp.where(offsets >= 0, jnp.exp(-rate * jnp.maximum(offsets, 0.0)), 0.0) * scale
        scores = lax.dot_general(query_one, key_one, over_cols, preferred_element_type=jnp.float32)
        weights = (scores * damping).astype(jnp.bfloat16)
        grad_scores = lax.dot_general(
            upstream_one, value_one, over_cols, preferred_element_type=jnp.float32
        )
        gweights = (grad_scores * damping).astype(jnp.bfloat16)
        leading_scale = (scale * jnp.exp(-rate * position))[:, None]
        trailing_scale = (scale * jnp.exp(-rate * (seg_len - 1.0 - position)))[:, None]
        attended = jnp.dot(weights, value_one, preferred_element_type=jnp.float32)
        attended = attended + leading_scale * jnp.dot(
            query_one.astype(jnp.float32), start_state, precision=greatest_precision
        )
        query_gradient = jnp.dot(gweights, key_one, preferred_element_type=jnp.float32)
        query_gradient = query_gradient + leading_scale * lax.dot_general(
            upstream_one.astype(jnp.float32), start_state, over_cols, precision=greatest_precision
        )
        key_gradient = lax.dot_general(
            gweights, query_one, over_rows, preferred_element_type=jnp.float32
        )
        key_gradient = key_gradient + trailing_scale * lax.dot_general(
            value_one.astype(jnp.float32), end_state, over_cols, precision=greatest_precision
        )
        value_gradient = lax.dot_general(
            weights, upstream_one, over_rows, preferred_element_type=jnp.float32
        )
        value_gradient = value_gradient + trailing_scale * jnp.dot(
            key_one.astype(jnp.float32), end_state, precision=greatest_precision
        )
        return (
            attended.astype(jnp.bfloat16),
            query_gradient.astype(jnp.bfloat16),
            key_gradient.astype(jnp.bfloat16),
            value_gradient.astype(jnp.bfloat16),
        )

    head_outputs = [head_work(index) for index in range(num_heads)]
    results = tuple(
        (
            jnp.stack([single[member] for single in head_outputs], axis=1).reshape(
                seg_len, num_heads * head_size
            )
            for member in range(4)
        )
    )
    return lax.all_to_all(results, "exp", split_axis=0, concat_axis=1, tiled=True)


def solution(mesh):
    placed = (P("seq", "exp"), P("seq", "exp"), P("seq", "exp"), P("seq", "exp"), P("exp"))
    return jax.shard_map(
        shards,
        mesh=mesh,
        in_specs=placed,
        out_specs=(
            P(("seq", "exp"), None),
            P(("seq", "exp"), None),
            P(("seq", "exp"), None),
            P(("seq", "exp"), None),
        ),
        check_vma=False,
    )
```

```python
import functools

import jax
import jax.numpy as jnp
from jax import lax
from jax.experimental import pallas as pl
from jax.experimental.pallas import tpu as pltpu
from jax.sharding import PartitionSpec as P


MESH = pl.DeviceIdType.MESH


def scan_kernel(n, near, far, w_ref, k_ref, q_ref, s_out, r_out, kx, qx, krecv, qrecv, sems):
    me = lax.axis_index("seq")
    ex = lax.axis_index("exp")
    heads = k_ref.shape[0]
    barrier = pltpu.get_barrier_semaphore()
    partners = sorted(set(near + [1, far]))
    for d in partners:
        for other in (me + d, me - d):
            @pl.when(jnp.logical_and(other >= 0, other < n))
            def _():
                pl.semaphore_signal(barrier, 1, device_id=(other, ex), device_id_type=MESH)
    peers = 0
    for d in partners:
        for other in (me + d, me - d):
            peers = peers + jnp.logical_and(other >= 0, other < n).astype(jnp.int32)
    pl.semaphore_wait(barrier, peers)

    def copy(src, dst, slot, other):
        return pltpu.make_async_remote_copy(
            src_ref=src, dst_ref=dst, send_sem=sems.at[0, slot], recv_sem=sems.at[1, slot],
            device_id=(lax.rem(other + n, n), ex), device_id_type=MESH,
        )

    sent = []
    kcur, qcur = k_ref, q_ref
    for r, d in enumerate(near):
        kc = copy(kcur, krecv.at[r], 2 * r, me + d)
        qc = copy(qcur, qrecv.at[r], 2 * r + 1, me - d)
        pl.when(me + d < n)(kc.start)
        pl.when(me - d >= 0)(qc.start)
        sent.append((kc, me + d < n))
        sent.append((qc, me - d >= 0))
        for cur, nxt, recv, cp, has in ((kcur, kx, krecv, kc, me - d >= 0), (qcur, qx, qrecv, qc, me + d < n)):
            @pl.when(has)
            def _():
                cp.wait_recv()
                for h in range(heads):
                    nxt[r, h] = cur[h] + w_ref[r * heads + h] * recv[r, h]

            @pl.when(jnp.logical_not(has))
            def _():
                nxt[r] = cur[...]
        kcur, qcur = kx.at[r], qx.at[r]
    last = len(near)
    finals = []
    for j, d in enumerate((1, far)):
        slot = 2 * (last + j)
        kc = copy(kcur, krecv.at[last + j], slot, me + d)
        qc = copy(qcur, qrecv.at[last + j], slot + 1, me - d)
        pl.when(me + d < n)(kc.start)
        pl.when(me - d >= 0)(qc.start)
        sent.append((kc, me + d < n))
        sent.append((qc, me - d >= 0))
        finals.append((kc, qc, d))
    s_out[...] = jnp.zeros_like(s_out)
    r_out[...] = jnp.zeros_like(r_out)
    for j, (kc, qc, d) in enumerate(finals):
        for cp, recv, out, has in ((kc, krecv, s_out, me - d >= 0), (qc, qrecv, r_out, me + d < n)):
            @pl.when(has)
            def _():
                cp.wait_recv()
                for h in range(heads):
                    scale = 1.0 if j == 0 else w_ref[last * heads + h]
                    out[h] = out[h] + scale * recv[last + j, h]
    for cp, cond in sent:
        pl.when(cond)(cp.wait_send)


def state_scan(dev_key, dev_query, rate_len, n):
    near = []
    d = 1
    while 2 * d < n:
        near.append(d)
        d *= 2
    far = d + 1
    heads = dev_key.shape[0]
    dists = jnp.asarray(near + [d], jnp.float32)
    weights = jnp.exp(-dists[:, None] * rate_len[None, :]).reshape(-1)
    nrecv = len(near) + 2
    body = functools.partial(scan_kernel, n, near, far)
    state = jax.ShapeDtypeStruct(dev_key.shape, jnp.float32)
    vspec = pl.BlockSpec(memory_space=pltpu.VMEM)
    return pl.pallas_call(
        body,
        out_shape=(state, state),
        in_specs=[pl.BlockSpec(memory_space=pltpu.SMEM), vspec, vspec],
        out_specs=(vspec, vspec),
        scratch_shapes=[
            pltpu.VMEM((len(near),) + dev_key.shape, jnp.float32),
            pltpu.VMEM((len(near),) + dev_key.shape, jnp.float32),
            pltpu.VMEM((nrecv,) + dev_key.shape, jnp.float32),
            pltpu.VMEM((nrecv,) + dev_key.shape, jnp.float32),
            pltpu.SemaphoreType.DMA((2, 2 * nrecv)),
        ],
        compiler_params=pltpu.CompilerParams(collective_id=0, has_side_effects=True),
    )(weights, dev_key, dev_query)


def fused_kernel(scal_ref, q_ref, k_ref, v_ref, do_ref, s_ref, r_ref, o0, o1, o2, o3,
                 stage, wts, gwts, send_sems, recv_sems, local_sems):
    outs = (o0, o1, o2, o3)
    seq = lax.axis_index("seq")
    me = lax.axis_index("exp")
    ne = lax.axis_size("exp")
    length, width = q_ref.shape
    heads = scal_ref.shape[0] // 2
    hd = width // heads
    slab = length // ne
    blk = min(256, length)
    nblk = length // blk
    hi = lax.Precision.HIGHEST
    f32 = jnp.float32

    barrier = pltpu.get_barrier_semaphore()
    for j in range(1, ne):
        pl.semaphore_signal(barrier, 1, device_id=(seq, lax.rem(me + j, ne)), device_id_type=MESH)
    pl.semaphore_wait(barrier, ne - 1)

    def cols(h):
        return pl.ds(h * hd, hd)

    for h in range(heads):
        rate = scal_ref[h]
        scale = scal_ref[heads + h]
        qh = q_ref[:, cols(h)]
        kh = k_ref[:, cols(h)]
        vh = v_ref[:, cols(h)]
        dh = do_ref[:, cols(h)]
        for b in range(nblk):
            rows = pl.ds(b * blk, blk)
            i = (lax.broadcasted_iota(jnp.int32, (blk, length), 0) + b * blk).astype(f32)
            jj = lax.broadcasted_iota(jnp.int32, (blk, length), 1).astype(f32)
            off = i - jj
            damp = jnp.where(off >= 0, jnp.exp(-rate * jnp.maximum(off, 0.0)), 0.0) * scale
            sc = lax.dot_general(qh[b * blk:(b + 1) * blk], kh, (((1,), (1,)), ((), ())), preferred_element_type=f32)
            wts[h, rows, :] = (sc * damp).astype(jnp.bfloat16)
            gs = lax.dot_general(dh[b * blk:(b + 1) * blk], vh, (((1,), (1,)), ((), ())), preferred_element_type=f32)
            gwts[h, rows, :] = (gs * damp).astype(jnp.bfloat16)

    def send(o):
        for j in range(1, ne):
            peer = lax.rem(me + j, ne)
            pltpu.make_async_remote_copy(
                src_ref=stage.at[o, pl.ds(pl.multiple_of(peer * slab, slab), slab), :],
                dst_ref=outs[o].at[:, pl.ds(pl.multiple_of(me * width, width), width)],
                send_sem=send_sems.at[o, j], recv_sem=recv_sems.at[o, j],
                device_id=(seq, peer), device_id_type=MESH,
            ).start()
        pltpu.make_async_copy(
            stage.at[o, pl.ds(pl.multiple_of(me * slab, slab), slab), :],
            outs[o].at[:, pl.ds(pl.multiple_of(me * width, width), width)],
            local_sems.at[o],
        ).start()

    def pos(b):
        return (lax.broadcasted_iota(jnp.int32, (blk, 1), 0) + b * blk).astype(f32)

    for o in range(4):
        for h in range(heads):
            rate = scal_ref[h]
            scale = scal_ref[heads + h]
            for b in range(nblk):
                rows = pl.ds(b * blk, blk)
                if o == 0:
                    lead = scale * jnp.exp(-rate * pos(b))
                    res = jnp.dot(wts[h, rows, :], v_ref[:, cols(h)], preferred_element_type=f32)
                    res = res + lead * jnp.dot(q_ref[rows, cols(h)].astype(f32), s_ref[h], precision=hi, preferred_element_type=f32)
                elif o == 1:
                    lead = scale * jnp.exp(-rate * pos(b))
                    res = jnp.dot(gwts[h, rows, :], k_ref[:, cols(h)], preferred_element_type=f32)
                    res = res + lead * lax.dot_general(do_ref[rows, cols(h)].astype(f32), s_ref[h], (((1,), (1,)), ((), ())), precision=hi, preferred_element_type=f32)
                elif o == 2:
                    trail = scale * jnp.exp(-rate * (length - 1.0 - pos(b)))
                    res = lax.dot_general(gwts[h, :, rows], q_ref[:, cols(h)], (((0,), (0,)), ((), ())), preferred_element_type=f32)
                    res = res + trail * lax.dot_general(v_ref[rows, cols(h)].astype(f32), r_ref[h], (((1,), (1,)), ((), ())), precision=hi, preferred_element_type=f32)
                else:
                    trail = scale * jnp.exp(-rate * (length - 1.0 - pos(b)))
                    res = lax.dot_general(wts[h, :, rows], do_ref[:, cols(h)], (((0,), (0,)), ((), ())), preferred_element_type=f32)
                    res = res + trail * jnp.dot(k_ref[rows, cols(h)].astype(f32), r_ref[h], precision=hi, preferred_element_type=f32)
                stage[o, rows, cols(h)] = res.astype(jnp.bfloat16)
        send(o)

    for o in range(4):
        for j in range(1, ne):
            cp = pltpu.make_async_remote_copy(
                src_ref=stage.at[o, pl.ds(0, slab), :],
                dst_ref=outs[o].at[:, pl.ds(0, width)],
                send_sem=send_sems.at[o, j], recv_sem=recv_sems.at[o, j],
                device_id=(seq, lax.rem(me + j, ne)), device_id_type=MESH,
            )
            cp.wait_send()
            cp.wait_recv()
        pltpu.make_async_copy(
            stage.at[o, pl.ds(0, slab), :], outs[o].at[:, pl.ds(0, width)], local_sems.at[o]
        ).wait()


def shards(query_tok, key_tok, value_tok, grad_out, decay_rate):
    seg_len = query_tok.shape[0]
    num_heads = decay_rate.shape[0]
    head_size = query_tok.shape[1] // num_heads
    ne = lax.axis_size("exp")
    total_len = seg_len * lax.axis_size("seq")
    scale_head = jnp.sqrt((2.0 * decay_rate + 2.0 / total_len) / head_size)
    shape_three = (seg_len, num_heads, head_size)
    query_heads = query_tok.reshape(shape_three)
    key_heads = key_tok.reshape(shape_three)
    value_heads = value_tok.reshape(shape_three)
    upstream = grad_out.reshape(shape_three)
    position = jnp.arange(seg_len, dtype=jnp.float32)
    to_end = jnp.exp(-decay_rate[None, :] * (seg_len - position[:, None]))
    from_start = jnp.exp(-decay_rate[None, :] * (position[:, None] + 1.0))
    key_product = (key_heads * to_end[:, :, None]).astype(jnp.bfloat16)
    query_product = (query_heads * from_start[:, :, None]).astype(jnp.bfloat16)
    dev_key = jnp.einsum(
        "ihd,ihe->hde", key_product, value_heads, preferred_element_type=jnp.float32
    )
    dev_query = jnp.einsum(
        "ihd,ihe->hde", query_product, upstream, preferred_element_type=jnp.float32
    )
    rate_len = decay_rate * seg_len
    incoming, outgoing = state_scan(dev_key, dev_query, rate_len, lax.axis_size("seq"))
    scalars = jnp.concatenate([decay_rate, scale_head]).astype(jnp.float32)
    width = query_tok.shape[1]
    slab = seg_len // ne
    out = jax.ShapeDtypeStruct((slab, ne * width), jnp.bfloat16)
    vspec = pl.BlockSpec(memory_space=pltpu.VMEM)
    anyspec = pl.BlockSpec(memory_space=pl.ANY)
    return pl.pallas_call(
        fused_kernel,
        out_shape=(out, out, out, out),
        in_specs=[pl.BlockSpec(memory_space=pltpu.SMEM)] + [vspec] * 6,
        out_specs=(anyspec, anyspec, anyspec, anyspec),
        scratch_shapes=[
            pltpu.VMEM((4, seg_len, width), jnp.bfloat16),
            pltpu.VMEM((num_heads, seg_len, seg_len), jnp.bfloat16),
            pltpu.VMEM((num_heads, seg_len, seg_len), jnp.bfloat16),
            pltpu.SemaphoreType.DMA((4, ne)),
            pltpu.SemaphoreType.DMA((4, ne)),
            pltpu.SemaphoreType.DMA((4,)),
        ],
        compiler_params=pltpu.CompilerParams(
            collective_id=1, has_side_effects=True, vmem_limit_bytes=48 * 1024 * 1024
        ),
    )(scalars, query_tok, key_tok, value_tok, grad_out, incoming, outgoing)


def solution(mesh):
    placed = (P("seq", "exp"), P("seq", "exp"), P("seq", "exp"), P("seq", "exp"), P("exp"))
    return jax.shard_map(
        shards,
        mesh=mesh,
        in_specs=placed,
        out_specs=(
            P(("seq", "exp"), None),
            P(("seq", "exp"), None),
            P(("seq", "exp"), None),
            P(("seq", "exp"), None),
        ),
        check_vma=False,
    )
```

```python
import functools

import jax
import jax.numpy as jnp
from jax import lax
from jax.experimental import pallas as pl
from jax.experimental.pallas import tpu as pltpu
from jax.sharding import PartitionSpec as P


MESH = pl.DeviceIdType.MESH


def whole_kernel(n, near, far, w_ref, scal_ref, q_ref, k_ref, v_ref, do_ref, dk_ref, dq_ref,
                 o0, o1, o2, o3, kx, qx, krecv, qrecv, s_acc, r_acc, intra, stage, wts, gwts,
                 scan_sems, send_sems, recv_sems, local_sems):
    outs = (o0, o1, o2, o3)
    me_s = lax.axis_index("seq")
    me = lax.axis_index("exp")
    ne = lax.axis_size("exp")
    length, width = q_ref.shape
    heads = scal_ref.shape[0] // 2
    hd = width // heads
    slab = length // ne
    blk = min(256, length)
    nblk = length // blk
    hi = lax.Precision.HIGHEST
    f32 = jnp.float32
    nt = (((1,), (1,)), ((), ()))
    tn = (((0,), (0,)), ((), ()))

    barrier = pltpu.get_barrier_semaphore()
    partners = sorted(set(near + [1, far]))
    peers = ne - 1
    for d in partners:
        for other in (me_s + d, me_s - d):
            @pl.when(jnp.logical_and(other >= 0, other < n))
            def _():
                pl.semaphore_signal(barrier, 1, device_id=(other, me), device_id_type=MESH)
            peers = peers + jnp.logical_and(other >= 0, other < n).astype(jnp.int32)
    for j in range(1, ne):
        pl.semaphore_signal(barrier, 1, device_id=(me_s, lax.rem(me + j, ne)), device_id_type=MESH)
    pl.semaphore_wait(barrier, peers)

    def cols(h):
        return pl.ds(h * hd, hd)

    def weights_task(h):
        def run():
            rate = scal_ref[h]
            scale = scal_ref[heads + h]
            qh = q_ref[:, cols(h)]
            kh = k_ref[:, cols(h)]
            vh = v_ref[:, cols(h)]
            dh = do_ref[:, cols(h)]
            for b in range(nblk):
                rows = pl.ds(b * blk, blk)
                i = (lax.broadcasted_iota(jnp.int32, (blk, length), 0) + b * blk).astype(f32)
                jj = lax.broadcasted_iota(jnp.int32, (blk, length), 1).astype(f32)
                off = i - jj
                damp = jnp.where(off >= 0, jnp.exp(-rate * jnp.maximum(off, 0.0)), 0.0) * scale
                sc = lax.dot_general(qh[b * blk:(b + 1) * blk], kh, nt, preferred_element_type=f32)
                wts[h, rows, :] = (sc * damp).astype(jnp.bfloat16)
                gs = lax.dot_general(dh[b * blk:(b + 1) * blk], vh, nt, preferred_element_type=f32)
                gwts[h, rows, :] = (gs * damp).astype(jnp.bfloat16)
        return run

    def intra_task(h, o):
        def run():
            for b in range(nblk):
                rows = pl.ds(b * blk, blk)
                if o == 0:
                    res = jnp.dot(wts[h, rows, :], v_ref[:, cols(h)], preferred_element_type=f32)
                elif o == 1:
                    res = jnp.dot(gwts[h, rows, :], k_ref[:, cols(h)], preferred_element_type=f32)
                elif o == 2:
                    res = lax.dot_general(gwts[h, :, rows], q_ref[:, cols(h)], tn, preferred_element_type=f32)
                else:
                    res = lax.dot_general(wts[h, :, rows], do_ref[:, cols(h)], tn, preferred_element_type=f32)
                intra[o, rows, cols(h)] = res
        return run

    tasks = []
    for h in range(heads):
        tasks.append(weights_task(h))
        tasks.extend(intra_task(h, o) for o in range(4))

    def copy(src, dst, slot, other):
        return pltpu.make_async_remote_copy(
            src_ref=src, dst_ref=dst, send_sem=scan_sems.at[0, slot], recv_sem=scan_sems.at[1, slot],
            device_id=(lax.rem(other + n, n), me), device_id_type=MESH,
        )

    nround = len(near) + 1
    per_round = -(-len(tasks) // nround)
    sent = []
    kcur, qcur = dk_ref, dq_ref
    for r, d in enumerate(near):
        kc = copy(kcur, krecv.at[r], 2 * r, me_s + d)
        qc = copy(qcur, qrecv.at[r], 2 * r + 1, me_s - d)
        pl.when(me_s + d < n)(kc.start)
        pl.when(me_s - d >= 0)(qc.start)
        sent.append((kc, me_s + d < n))
        sent.append((qc, me_s - d >= 0))
        for task in tasks[r * per_round:(r + 1) * per_round]:
            task()
        for cur, nxt, recv, cp, has in ((kcur, kx, krecv, kc, me_s - d >= 0), (qcur, qx, qrecv, qc, me_s + d < n)):
            @pl.when(has)
            def _():
                cp.wait_recv()
                for h in range(heads):
                    nxt[r, h] = cur[h] + w_ref[r * heads + h] * recv[r, h]

            @pl.when(jnp.logical_not(has))
            def _():
                nxt[r] = cur[...]
        kcur, qcur = kx.at[r], qx.at[r]
    last = len(near)
    finals = []
    for j, d in enumerate((1, far)):
        slot = 2 * (last + j)
        kc = copy(kcur, krecv.at[last + j], slot, me_s + d)
        qc = copy(qcur, qrecv.at[last + j], slot + 1, me_s - d)
        pl.when(me_s + d < n)(kc.start)
        pl.when(me_s - d >= 0)(qc.start)
        sent.append((kc, me_s + d < n))
        sent.append((qc, me_s - d >= 0))
        finals.append((kc, qc, d))
    for task in tasks[last * per_round:]:
        task()
    s_acc[...] = jnp.zeros_like(s_acc)
    r_acc[...] = jnp.zeros_like(r_acc)
    for j, (kc, qc, d) in enumerate(finals):
        for cp, recv, acc, has in ((kc, krecv, s_acc, me_s - d >= 0), (qc, qrecv, r_acc, me_s + d < n)):
            @pl.when(has)
            def _():
                cp.wait_recv()
                for h in range(heads):
                    scale = 1.0 if j == 0 else w_ref[last * heads + h]
                    acc[h] = acc[h] + scale * recv[last + j, h]

    def send(o):
        for j in range(1, ne):
            peer = lax.rem(me + j, ne)
            pltpu.make_async_remote_copy(
                src_ref=stage.at[o, pl.ds(pl.multiple_of(peer * slab, slab), slab), :],
                dst_ref=outs[o].at[:, pl.ds(pl.multiple_of(me * width, width), width)],
                send_sem=send_sems.at[o, j], recv_sem=recv_sems.at[o, j],
                device_id=(me_s, peer), device_id_type=MESH,
            ).start()
        pltpu.make_async_copy(
            stage.at[o, pl.ds(pl.multiple_of(me * slab, slab), slab), :],
            outs[o].at[:, pl.ds(pl.multiple_of(me * width, width), width)],
            local_sems.at[o],
        ).start()

    def pos(b):
        return (lax.broadcasted_iota(jnp.int32, (blk, 1), 0) + b * blk).astype(f32)

    for o in range(4):
        for h in range(heads):
            rate = scal_ref[h]
            scale = scal_ref[heads + h]
            for b in range(nblk):
                rows = pl.ds(b * blk, blk)
                if o == 0:
                    lead = scale * jnp.exp(-rate * pos(b))
                    extra = lead * jnp.dot(q_ref[rows, cols(h)].astype(f32), s_acc[h], precision=hi, preferred_element_type=f32)
                elif o == 1:
                    lead = scale * jnp.exp(-rate * pos(b))
                    extra = lead * lax.dot_general(do_ref[rows, cols(h)].astype(f32), s_acc[h], nt, precision=hi, preferred_element_type=f32)
                elif o == 2:
                    trail = scale * jnp.exp(-rate * (length - 1.0 - pos(b)))
                    extra = trail * lax.dot_general(v_ref[rows, cols(h)].astype(f32), r_acc[h], nt, precision=hi, preferred_element_type=f32)
                else:
                    trail = scale * jnp.exp(-rate * (length - 1.0 - pos(b)))
                    extra = trail * jnp.dot(k_ref[rows, cols(h)].astype(f32), r_acc[h], precision=hi, preferred_element_type=f32)
                stage[o, rows, cols(h)] = (intra[o, rows, cols(h)] + extra).astype(jnp.bfloat16)
        send(o)

    for cp, cond in sent:
        pl.when(cond)(cp.wait_send)
    for o in range(4):
        for j in range(1, ne):
            cp = pltpu.make_async_remote_copy(
                src_ref=stage.at[o, pl.ds(0, slab), :],
                dst_ref=outs[o].at[:, pl.ds(0, width)],
                send_sem=send_sems.at[o, j], recv_sem=recv_sems.at[o, j],
                device_id=(me_s, lax.rem(me + j, ne)), device_id_type=MESH,
            )
            cp.wait_send()
            cp.wait_recv()
        pltpu.make_async_copy(
            stage.at[o, pl.ds(0, slab), :], outs[o].at[:, pl.ds(0, width)], local_sems.at[o]
        ).wait()


def shards(query_tok, key_tok, value_tok, grad_out, decay_rate):
    seg_len = query_tok.shape[0]
    num_heads = decay_rate.shape[0]
    head_size = query_tok.shape[1] // num_heads
    ne = lax.axis_size("exp")
    total_len = seg_len * lax.axis_size("seq")
    scale_head = jnp.sqrt((2.0 * decay_rate + 2.0 / total_len) / head_size)
    shape_three = (seg_len, num_heads, head_size)
    query_heads = query_tok.reshape(shape_three)
    key_heads = key_tok.reshape(shape_three)
    value_heads = value_tok.reshape(shape_three)
    upstream = grad_out.reshape(shape_three)
    position = jnp.arange(seg_len, dtype=jnp.float32)
    to_end = jnp.exp(-decay_rate[None, :] * (seg_len - position[:, None]))
    from_start = jnp.exp(-decay_rate[None, :] * (position[:, None] + 1.0))
    key_product = (key_heads * to_end[:, :, None]).astype(jnp.bfloat16)
    query_product = (query_heads * from_start[:, :, None]).astype(jnp.bfloat16)
    dev_key = jnp.einsum(
        "ihd,ihe->hde", key_product, value_heads, preferred_element_type=jnp.float32
    )
    dev_query = jnp.einsum(
        "ihd,ihe->hde", query_product, upstream, preferred_element_type=jnp.float32
    )
    rate_len = decay_rate * seg_len
    n = lax.axis_size("seq")
    near = []
    d = 1
    while 2 * d < n:
        near.append(d)
        d *= 2
    far = d + 1
    dists = jnp.asarray(near + [d], jnp.float32)
    weights = jnp.exp(-dists[:, None] * rate_len[None, :]).reshape(-1)
    nrecv = len(near) + 2
    scalars = jnp.concatenate([decay_rate, scale_head]).astype(jnp.float32)
    width = query_tok.shape[1]
    slab = seg_len // ne
    out = jax.ShapeDtypeStruct((slab, ne * width), jnp.bfloat16)
    smem = pl.BlockSpec(memory_space=pltpu.SMEM)
    vspec = pl.BlockSpec(memory_space=pltpu.VMEM)
    anyspec = pl.BlockSpec(memory_space=pl.ANY)
    st = dev_key.shape
    return pl.pallas_call(
        functools.partial(whole_kernel, n, near, far),
        out_shape=(out, out, out, out),
        in_specs=[smem, smem] + [vspec] * 6,
        out_specs=(anyspec, anyspec, anyspec, anyspec),
        scratch_shapes=[
            pltpu.VMEM((len(near),) + st, jnp.float32),
            pltpu.VMEM((len(near),) + st, jnp.float32),
            pltpu.VMEM((nrecv,) + st, jnp.float32),
            pltpu.VMEM((nrecv,) + st, jnp.float32),
            pltpu.VMEM(st, jnp.float32),
            pltpu.VMEM(st, jnp.float32),
            pltpu.VMEM((4, seg_len, width), jnp.float32),
            pltpu.VMEM((4, seg_len, width), jnp.bfloat16),
            pltpu.VMEM((num_heads, seg_len, seg_len), jnp.bfloat16),
            pltpu.VMEM((num_heads, seg_len, seg_len), jnp.bfloat16),
            pltpu.SemaphoreType.DMA((2, 2 * nrecv)),
            pltpu.SemaphoreType.DMA((4, ne)),
            pltpu.SemaphoreType.DMA((4, ne)),
            pltpu.SemaphoreType.DMA((4,)),
        ],
        compiler_params=pltpu.CompilerParams(
            collective_id=0, has_side_effects=True, vmem_limit_bytes=56 * 1024 * 1024
        ),
    )(weights, scalars, query_tok, key_tok, value_tok, grad_out, dev_key, dev_query)


def solution(mesh):
    placed = (P("seq", "exp"), P("seq", "exp"), P("seq", "exp"), P("seq", "exp"), P("exp"))
    return jax.shard_map(
        shards,
        mesh=mesh,
        in_specs=placed,
        out_specs=(
            P(("seq", "exp"), None),
            P(("seq", "exp"), None),
            P(("seq", "exp"), None),
            P(("seq", "exp"), None),
        ),
        check_vma=False,
    )
```

```python
import functools

import jax
import jax.numpy as jnp
from jax import lax
from jax.experimental import pallas as pl
from jax.experimental.pallas import tpu as pltpu
from jax.sharding import PartitionSpec as P


MESH = pl.DeviceIdType.MESH


def whole_kernel(n, near, far, w_ref, scal_ref, q_ref, k_ref, v_ref, do_ref, dk_ref, dq_ref,
                 o0, o1, o2, o3, kx, qx, krecv, qrecv, s_acc, r_acc, intra, stage, wts, gwts,
                 scan_sems, send_sems, recv_sems, local_sems):
    outs = (o0, o1, o2, o3)
    me_s = lax.axis_index("seq")
    me = lax.axis_index("exp")
    ne = lax.axis_size("exp")
    length, width = q_ref.shape
    heads = scal_ref.shape[0] // 2
    hd = width // heads
    slab = length // ne
    blk = min(256, length)
    nblk = length // blk
    hi = lax.Precision.HIGHEST
    f32 = jnp.float32
    nt = (((1,), (1,)), ((), ()))
    tn = (((0,), (0,)), ((), ()))

    barrier = pltpu.get_barrier_semaphore()
    partners = sorted(set(near + [1, far]))
    peers = ne - 1
    for d in partners:
        for other in (me_s + d, me_s - d):
            @pl.when(jnp.logical_and(other >= 0, other < n))
            def _():
                pl.semaphore_signal(barrier, 1, device_id=(other, me), device_id_type=MESH)
            peers = peers + jnp.logical_and(other >= 0, other < n).astype(jnp.int32)
    for j in range(1, ne):
        pl.semaphore_signal(barrier, 1, device_id=(me_s, lax.rem(me + j, ne)), device_id_type=MESH)
    pl.semaphore_wait(barrier, peers)

    def cols(h):
        return pl.ds(h * hd, hd)

    def weights_task(h):
        def run():
            rate = scal_ref[h]
            scale = scal_ref[heads + h]
            qh = q_ref[:, cols(h)]
            kh = k_ref[:, cols(h)]
            vh = v_ref[:, cols(h)]
            dh = do_ref[:, cols(h)]
            for b in range(nblk):
                rows = pl.ds(b * blk, blk)
                i = (lax.broadcasted_iota(jnp.int32, (blk, length), 0) + b * blk).astype(f32)
                jj = lax.broadcasted_iota(jnp.int32, (blk, length), 1).astype(f32)
                off = i - jj
                damp = jnp.where(off >= 0, jnp.exp(-rate * jnp.maximum(off, 0.0)), 0.0) * scale
                sc = lax.dot_general(qh[b * blk:(b + 1) * blk], kh, nt, preferred_element_type=f32)
                wts[h, rows, :] = (sc * damp).astype(jnp.bfloat16)
                gs = lax.dot_general(dh[b * blk:(b + 1) * blk], vh, nt, preferred_element_type=f32)
                gwts[h, rows, :] = (gs * damp).astype(jnp.bfloat16)
        return run

    def intra_task(h, o):
        def run():
            for b in range(nblk):
                rows = pl.ds(b * blk, blk)
                if o == 0:
                    res = jnp.dot(wts[h, rows, :], v_ref[:, cols(h)], preferred_element_type=f32)
                elif o == 1:
                    res = jnp.dot(gwts[h, rows, :], k_ref[:, cols(h)], preferred_element_type=f32)
                elif o == 2:
                    res = lax.dot_general(gwts[h, :, rows], q_ref[:, cols(h)], tn, preferred_element_type=f32)
                else:
                    res = lax.dot_general(wts[h, :, rows], do_ref[:, cols(h)], tn, preferred_element_type=f32)
                intra[o, rows, cols(h)] = res
        return run

    def copy(src, dst, h, slot, other):
        return pltpu.make_async_remote_copy(
            src_ref=src, dst_ref=dst, send_sem=scan_sems.at[0, h, slot], recv_sem=scan_sems.at[1, h, slot],
            device_id=(lax.rem(other + n, n), me), device_id_type=MESH,
        )

    def send(o, h):
        for j in range(1, ne):
            peer = lax.rem(me + j, ne)
            pltpu.make_async_remote_copy(
                src_ref=stage.at[o, pl.ds(pl.multiple_of(peer * slab, slab), slab), cols(h)],
                dst_ref=outs[o].at[:, pl.ds(pl.multiple_of(me * width + h * hd, hd), hd)],
                send_sem=send_sems.at[o, h, j], recv_sem=recv_sems.at[o, h, j],
                device_id=(me_s, peer), device_id_type=MESH,
            ).start()
        pltpu.make_async_copy(
            stage.at[o, pl.ds(pl.multiple_of(me * slab, slab), slab), cols(h)],
            outs[o].at[:, pl.ds(pl.multiple_of(me * width + h * hd, hd), hd)],
            local_sems.at[o, h],
        ).start()

    def pos(b):
        return (lax.broadcasted_iota(jnp.int32, (blk, 1), 0) + b * blk).astype(f32)

    nround = len(near) + 1
    sent = []
    last = len(near)
    for h in range(heads):
        mine = [weights_task(h)] + [intra_task(h, o) for o in range(4)]
        per_round = -(-len(mine) // nround)
        kcur, qcur = dk_ref.at[h], dq_ref.at[h]
        for r, d in enumerate(near):
            kc = copy(kcur, krecv.at[r, h], h, 2 * r, me_s + d)
            qc = copy(qcur, qrecv.at[r, h], h, 2 * r + 1, me_s - d)
            pl.when(me_s + d < n)(kc.start)
            pl.when(me_s - d >= 0)(qc.start)
            sent.append((kc, me_s + d < n))
            sent.append((qc, me_s - d >= 0))
            for task in mine[r * per_round:(r + 1) * per_round]:
                task()
            for cur, nxt, recv, cp, has in ((kcur, kx, krecv, kc, me_s - d >= 0), (qcur, qx, qrecv, qc, me_s + d < n)):
                @pl.when(has)
                def _():
                    cp.wait_recv()
                    nxt[r, h] = cur[...] + w_ref[r * heads + h] * recv[r, h]

                @pl.when(jnp.logical_not(has))
                def _():
                    nxt[r, h] = cur[...]
            kcur, qcur = kx.at[r, h], qx.at[r, h]
        finals = []
        for j, d in enumerate((1, far)):
            slot = 2 * (last + j)
            kc = copy(kcur, krecv.at[last + j, h], h, slot, me_s + d)
            qc = copy(qcur, qrecv.at[last + j, h], h, slot + 1, me_s - d)
            pl.when(me_s + d < n)(kc.start)
            pl.when(me_s - d >= 0)(qc.start)
            sent.append((kc, me_s + d < n))
            sent.append((qc, me_s - d >= 0))
            finals.append((kc, qc, d))
        for task in mine[last * per_round:]:
            task()
        s_acc[h] = jnp.zeros((hd, hd), f32)
        r_acc[h] = jnp.zeros((hd, hd), f32)
        for j, (kc, qc, d) in enumerate(finals):
            for cp, recv, acc, has in ((kc, krecv, s_acc, me_s - d >= 0), (qc, qrecv, r_acc, me_s + d < n)):
                @pl.when(has)
                def _():
                    cp.wait_recv()
                    scale = 1.0 if j == 0 else w_ref[last * heads + h]
                    acc[h] = acc[h] + scale * recv[last + j, h]

        rate = scal_ref[h]
        scale = scal_ref[heads + h]
        for o in range(4):
            for b in range(nblk):
                rows = pl.ds(b * blk, blk)
                if o == 0:
                    lead = scale * jnp.exp(-rate * pos(b))
                    extra = lead * jnp.dot(q_ref[rows, cols(h)].astype(f32), s_acc[h], precision=hi, preferred_element_type=f32)
                elif o == 1:
                    lead = scale * jnp.exp(-rate * pos(b))
                    extra = lead * lax.dot_general(do_ref[rows, cols(h)].astype(f32), s_acc[h], nt, precision=hi, preferred_element_type=f32)
                elif o == 2:
                    trail = scale * jnp.exp(-rate * (length - 1.0 - pos(b)))
                    extra = trail * lax.dot_general(v_ref[rows, cols(h)].astype(f32), r_acc[h], nt, precision=hi, preferred_element_type=f32)
                else:
                    trail = scale * jnp.exp(-rate * (length - 1.0 - pos(b)))
                    extra = trail * jnp.dot(k_ref[rows, cols(h)].astype(f32), r_acc[h], precision=hi, preferred_element_type=f32)
                stage[o, rows, cols(h)] = (intra[o, rows, cols(h)] + extra).astype(jnp.bfloat16)
            send(o, h)

    for cp, cond in sent:
        pl.when(cond)(cp.wait_send)
    for o in range(4):
        for h in range(heads):
            for j in range(1, ne):
                cp = pltpu.make_async_remote_copy(
                    src_ref=stage.at[o, pl.ds(0, slab), cols(h)],
                    dst_ref=outs[o].at[:, pl.ds(h * hd, hd)],
                    send_sem=send_sems.at[o, h, j], recv_sem=recv_sems.at[o, h, j],
                    device_id=(me_s, lax.rem(me + j, ne)), device_id_type=MESH,
                )
                cp.wait_send()
                cp.wait_recv()
            pltpu.make_async_copy(
                stage.at[o, pl.ds(0, slab), cols(h)], outs[o].at[:, pl.ds(h * hd, hd)], local_sems.at[o, h]
            ).wait()


def shards(query_tok, key_tok, value_tok, grad_out, decay_rate):
    seg_len = query_tok.shape[0]
    num_heads = decay_rate.shape[0]
    head_size = query_tok.shape[1] // num_heads
    ne = lax.axis_size("exp")
    total_len = seg_len * lax.axis_size("seq")
    scale_head = jnp.sqrt((2.0 * decay_rate + 2.0 / total_len) / head_size)
    shape_three = (seg_len, num_heads, head_size)
    query_heads = query_tok.reshape(shape_three)
    key_heads = key_tok.reshape(shape_three)
    value_heads = value_tok.reshape(shape_three)
    upstream = grad_out.reshape(shape_three)
    position = jnp.arange(seg_len, dtype=jnp.float32)
    to_end = jnp.exp(-decay_rate[None, :] * (seg_len - position[:, None]))
    from_start = jnp.exp(-decay_rate[None, :] * (position[:, None] + 1.0))
    key_product = (key_heads * to_end[:, :, None]).astype(jnp.bfloat16)
    query_product = (query_heads * from_start[:, :, None]).astype(jnp.bfloat16)
    dev_key = jnp.einsum(
        "ihd,ihe->hde", key_product, value_heads, preferred_element_type=jnp.float32
    )
    dev_query = jnp.einsum(
        "ihd,ihe->hde", query_product, upstream, preferred_element_type=jnp.float32
    )
    rate_len = decay_rate * seg_len
    n = lax.axis_size("seq")
    near = []
    d = 1
    while 2 * d < n:
        near.append(d)
        d *= 2
    far = d + 1
    dists = jnp.asarray(near + [d], jnp.float32)
    weights = jnp.exp(-dists[:, None] * rate_len[None, :]).reshape(-1)
    nrecv = len(near) + 2
    scalars = jnp.concatenate([decay_rate, scale_head]).astype(jnp.float32)
    width = query_tok.shape[1]
    slab = seg_len // ne
    out = jax.ShapeDtypeStruct((slab, ne * width), jnp.bfloat16)
    smem = pl.BlockSpec(memory_space=pltpu.SMEM)
    vspec = pl.BlockSpec(memory_space=pltpu.VMEM)
    anyspec = pl.BlockSpec(memory_space=pl.ANY)
    st = dev_key.shape
    return pl.pallas_call(
        functools.partial(whole_kernel, n, near, far),
        out_shape=(out, out, out, out),
        in_specs=[smem, smem] + [vspec] * 6,
        out_specs=(anyspec, anyspec, anyspec, anyspec),
        scratch_shapes=[
            pltpu.VMEM((len(near),) + st, jnp.float32),
            pltpu.VMEM((len(near),) + st, jnp.float32),
            pltpu.VMEM((nrecv,) + st, jnp.float32),
            pltpu.VMEM((nrecv,) + st, jnp.float32),
            pltpu.VMEM(st, jnp.float32),
            pltpu.VMEM(st, jnp.float32),
            pltpu.VMEM((4, seg_len, width), jnp.float32),
            pltpu.VMEM((4, seg_len, width), jnp.bfloat16),
            pltpu.VMEM((num_heads, seg_len, seg_len), jnp.bfloat16),
            pltpu.VMEM((num_heads, seg_len, seg_len), jnp.bfloat16),
            pltpu.SemaphoreType.DMA((2, num_heads, 2 * nrecv)),
            pltpu.SemaphoreType.DMA((4, num_heads, ne)),
            pltpu.SemaphoreType.DMA((4, num_heads, ne)),
            pltpu.SemaphoreType.DMA((4, num_heads)),
        ],
        compiler_params=pltpu.CompilerParams(
            collective_id=0, has_side_effects=True, vmem_limit_bytes=56 * 1024 * 1024
        ),
    )(weights, scalars, query_tok, key_tok, value_tok, grad_out, dev_key, dev_query)


def solution(mesh):
    placed = (P("seq", "exp"), P("seq", "exp"), P("seq", "exp"), P("seq", "exp"), P("exp"))
    return jax.shard_map(
        shards,
        mesh=mesh,
        in_specs=placed,
        out_specs=(
            P(("seq", "exp"), None),
            P(("seq", "exp"), None),
            P(("seq", "exp"), None),
            P(("seq", "exp"), None),
        ),
        check_vma=False,
    )
```

```python
import functools

import jax
import jax.numpy as jnp
from jax import lax
from jax.experimental import pallas as pl
from jax.experimental.pallas import tpu as pltpu
from jax.sharding import PartitionSpec as P


MESH = pl.DeviceIdType.MESH


def whole_kernel(n, near, far, w_ref, scal_ref, q_ref, k_ref, v_ref, do_ref,
                 o0, o1, o2, o3, dk_ref, dq_ref, kx, qx, krecv, qrecv, s_acc, r_acc, intra, stage, wts, gwts,
                 scan_sems, send_sems, recv_sems, local_sems):
    outs = (o0, o1, o2, o3)
    me_s = lax.axis_index("seq")
    me = lax.axis_index("exp")
    ne = lax.axis_size("exp")
    length, width = q_ref.shape
    heads = scal_ref.shape[0] // 2
    hd = width // heads
    slab = length // ne
    blk = min(256, length)
    nblk = length // blk
    hi = lax.Precision.HIGHEST
    f32 = jnp.float32
    nt = (((1,), (1,)), ((), ()))
    tn = (((0,), (0,)), ((), ()))

    def cols(h):
        return pl.ds(h * hd, hd)

    place = lax.broadcasted_iota(jnp.int32, (length, 1), 0).astype(f32)
    for h in range(heads):
        rate = scal_ref[h]
        keyed = (k_ref[:, cols(h)].astype(f32) * jnp.exp(-rate * (length - place))).astype(jnp.bfloat16)
        dk_ref[h] = lax.dot_general(keyed, v_ref[:, cols(h)], tn, preferred_element_type=f32)
        queried = (q_ref[:, cols(h)].astype(f32) * jnp.exp(-rate * (place + 1.0))).astype(jnp.bfloat16)
        dq_ref[h] = lax.dot_general(queried, do_ref[:, cols(h)], tn, preferred_element_type=f32)

    barrier = pltpu.get_barrier_semaphore()
    partners = sorted(set(near + [1, far]))
    peers = ne - 1
    for d in partners:
        for other in (me_s + d, me_s - d):
            @pl.when(jnp.logical_and(other >= 0, other < n))
            def _():
                pl.semaphore_signal(barrier, 1, device_id=(other, me), device_id_type=MESH)
            peers = peers + jnp.logical_and(other >= 0, other < n).astype(jnp.int32)
    for j in range(1, ne):
        pl.semaphore_signal(barrier, 1, device_id=(me_s, lax.rem(me + j, ne)), device_id_type=MESH)
    pl.semaphore_wait(barrier, peers)

    def weights_task(h):
        def run():
            rate = scal_ref[h]
            scale = scal_ref[heads + h]
            qh = q_ref[:, cols(h)]
            kh = k_ref[:, cols(h)]
            vh = v_ref[:, cols(h)]
            dh = do_ref[:, cols(h)]
            for b in range(nblk):
                rows = pl.ds(b * blk, blk)
                i = (lax.broadcasted_iota(jnp.int32, (blk, length), 0) + b * blk).astype(f32)
                jj = lax.broadcasted_iota(jnp.int32, (blk, length), 1).astype(f32)
                off = i - jj
                damp = jnp.where(off >= 0, jnp.exp(-rate * jnp.maximum(off, 0.0)), 0.0) * scale
                sc = lax.dot_general(qh[b * blk:(b + 1) * blk], kh, nt, preferred_element_type=f32)
                wts[h, rows, :] = (sc * damp).astype(jnp.bfloat16)
                gs = lax.dot_general(dh[b * blk:(b + 1) * blk], vh, nt, preferred_element_type=f32)
                gwts[h, rows, :] = (gs * damp).astype(jnp.bfloat16)
        return run

    def intra_task(h, o):
        def run():
            for b in range(nblk):
                rows = pl.ds(b * blk, blk)
                if o == 0:
                    res = jnp.dot(wts[h, rows, :], v_ref[:, cols(h)], preferred_element_type=f32)
                elif o == 1:
                    res = jnp.dot(gwts[h, rows, :], k_ref[:, cols(h)], preferred_element_type=f32)
                elif o == 2:
                    res = lax.dot_general(gwts[h, :, rows], q_ref[:, cols(h)], tn, preferred_element_type=f32)
                else:
                    res = lax.dot_general(wts[h, :, rows], do_ref[:, cols(h)], tn, preferred_element_type=f32)
                intra[o, rows, cols(h)] = res
        return run

    def copy(src, dst, h, slot, other):
        return pltpu.make_async_remote_copy(
            src_ref=src, dst_ref=dst, send_sem=scan_sems.at[0, h, slot], recv_sem=scan_sems.at[1, h, slot],
            device_id=(lax.rem(other + n, n), me), device_id_type=MESH,
        )

    def send(o, h):
        for j in range(1, ne):
            peer = lax.rem(me + j, ne)
            pltpu.make_async_remote_copy(
                src_ref=stage.at[o, pl.ds(pl.multiple_of(peer * slab, slab), slab), cols(h)],
                dst_ref=outs[o].at[:, pl.ds(pl.multiple_of(me * width + h * hd, hd), hd)],
                send_sem=send_sems.at[o, h, j], recv_sem=recv_sems.at[o, h, j],
                device_id=(me_s, peer), device_id_type=MESH,
            ).start()
        pltpu.make_async_copy(
            stage.at[o, pl.ds(pl.multiple_of(me * slab, slab), slab), cols(h)],
            outs[o].at[:, pl.ds(pl.multiple_of(me * width + h * hd, hd), hd)],
            local_sems.at[o, h],
        ).start()

    def pos(b):
        return (lax.broadcasted_iota(jnp.int32, (blk, 1), 0) + b * blk).astype(f32)

    nround = len(near) + 1
    sent = []
    last = len(near)
    for h in range(heads):
        mine = [weights_task(h)] + [intra_task(h, o) for o in range(4)]
        per_round = -(-len(mine) // nround)
        kcur, qcur = dk_ref.at[h], dq_ref.at[h]
        for r, d in enumerate(near):
            kc = copy(kcur, krecv.at[r, h], h, 2 * r, me_s + d)
            qc = copy(qcur, qrecv.at[r, h], h, 2 * r + 1, me_s - d)
            pl.when(me_s + d < n)(kc.start)
            pl.when(me_s - d >= 0)(qc.start)
            sent.append((kc, me_s + d < n))
            sent.append((qc, me_s - d >= 0))
            for task in mine[r * per_round:(r + 1) * per_round]:
                task()
            for cur, nxt, recv, cp, has in ((kcur, kx, krecv, kc, me_s - d >= 0), (qcur, qx, qrecv, qc, me_s + d < n)):
                @pl.when(has)
                def _():
                    cp.wait_recv()
                    nxt[r, h] = cur[...] + w_ref[r * heads + h] * recv[r, h]

                @pl.when(jnp.logical_not(has))
                def _():
                    nxt[r, h] = cur[...]
            kcur, qcur = kx.at[r, h], qx.at[r, h]
        finals = []
        for j, d in enumerate((1, far)):
            slot = 2 * (last + j)
            kc = copy(kcur, krecv.at[last + j, h], h, slot, me_s + d)
            qc = copy(qcur, qrecv.at[last + j, h], h, slot + 1, me_s - d)
            pl.when(me_s + d < n)(kc.start)
            pl.when(me_s - d >= 0)(qc.start)
            sent.append((kc, me_s + d < n))
            sent.append((qc, me_s - d >= 0))
            finals.append((kc, qc, d))
        for task in mine[last * per_round:]:
            task()
        s_acc[h] = jnp.zeros((hd, hd), f32)
        r_acc[h] = jnp.zeros((hd, hd), f32)
        for j, (kc, qc, d) in enumerate(finals):
            for cp, recv, acc, has in ((kc, krecv, s_acc, me_s - d >= 0), (qc, qrecv, r_acc, me_s + d < n)):
                @pl.when(has)
                def _():
                    cp.wait_recv()
                    scale = 1.0 if j == 0 else w_ref[last * heads + h]
                    acc[h] = acc[h] + scale * recv[last + j, h]

        rate = scal_ref[h]
        scale = scal_ref[heads + h]
        for o in range(4):
            for b in range(nblk):
                rows = pl.ds(b * blk, blk)
                if o == 0:
                    lead = scale * jnp.exp(-rate * pos(b))
                    extra = lead * jnp.dot(q_ref[rows, cols(h)].astype(f32), s_acc[h], precision=hi, preferred_element_type=f32)
                elif o == 1:
                    lead = scale * jnp.exp(-rate * pos(b))
                    extra = lead * lax.dot_general(do_ref[rows, cols(h)].astype(f32), s_acc[h], nt, precision=hi, preferred_element_type=f32)
                elif o == 2:
                    trail = scale * jnp.exp(-rate * (length - 1.0 - pos(b)))
                    extra = trail * lax.dot_general(v_ref[rows, cols(h)].astype(f32), r_acc[h], nt, precision=hi, preferred_element_type=f32)
                else:
                    trail = scale * jnp.exp(-rate * (length - 1.0 - pos(b)))
                    extra = trail * jnp.dot(k_ref[rows, cols(h)].astype(f32), r_acc[h], precision=hi, preferred_element_type=f32)
                stage[o, rows, cols(h)] = (intra[o, rows, cols(h)] + extra).astype(jnp.bfloat16)
            send(o, h)

    for cp, cond in sent:
        pl.when(cond)(cp.wait_send)
    for o in range(4):
        for h in range(heads):
            for j in range(1, ne):
                cp = pltpu.make_async_remote_copy(
                    src_ref=stage.at[o, pl.ds(0, slab), cols(h)],
                    dst_ref=outs[o].at[:, pl.ds(h * hd, hd)],
                    send_sem=send_sems.at[o, h, j], recv_sem=recv_sems.at[o, h, j],
                    device_id=(me_s, lax.rem(me + j, ne)), device_id_type=MESH,
                )
                cp.wait_send()
                cp.wait_recv()
            pltpu.make_async_copy(
                stage.at[o, pl.ds(0, slab), cols(h)], outs[o].at[:, pl.ds(h * hd, hd)], local_sems.at[o, h]
            ).wait()


def shards(query_tok, key_tok, value_tok, grad_out, decay_rate):
    seg_len = query_tok.shape[0]
    num_heads = decay_rate.shape[0]
    head_size = query_tok.shape[1] // num_heads
    ne = lax.axis_size("exp")
    total_len = seg_len * lax.axis_size("seq")
    scale_head = jnp.sqrt((2.0 * decay_rate + 2.0 / total_len) / head_size)
    rate_len = decay_rate * seg_len
    n = lax.axis_size("seq")
    near = []
    d = 1
    while 2 * d < n:
        near.append(d)
        d *= 2
    far = d + 1
    dists = jnp.asarray(near + [d], jnp.float32)
    weights = jnp.exp(-dists[:, None] * rate_len[None, :]).reshape(-1)
    nrecv = len(near) + 2
    scalars = jnp.concatenate([decay_rate, scale_head]).astype(jnp.float32)
    width = query_tok.shape[1]
    slab = seg_len // ne
    out = jax.ShapeDtypeStruct((slab, ne * width), jnp.bfloat16)
    smem = pl.BlockSpec(memory_space=pltpu.SMEM)
    vspec = pl.BlockSpec(memory_space=pltpu.VMEM)
    anyspec = pl.BlockSpec(memory_space=pl.ANY)
    st = (num_heads, head_size, head_size)
    return pl.pallas_call(
        functools.partial(whole_kernel, n, near, far),
        out_shape=(out, out, out, out),
        in_specs=[smem, smem] + [vspec] * 4,
        out_specs=(anyspec, anyspec, anyspec, anyspec),
        scratch_shapes=[
            pltpu.VMEM(st, jnp.float32),
            pltpu.VMEM(st, jnp.float32),
            pltpu.VMEM((len(near),) + st, jnp.float32),
            pltpu.VMEM((len(near),) + st, jnp.float32),
            pltpu.VMEM((nrecv,) + st, jnp.float32),
            pltpu.VMEM((nrecv,) + st, jnp.float32),
            pltpu.VMEM(st, jnp.float32),
            pltpu.VMEM(st, jnp.float32),
            pltpu.VMEM((4, seg_len, width), jnp.float32),
            pltpu.VMEM((4, seg_len, width), jnp.bfloat16),
            pltpu.VMEM((num_heads, seg_len, seg_len), jnp.bfloat16),
            pltpu.VMEM((num_heads, seg_len, seg_len), jnp.bfloat16),
            pltpu.SemaphoreType.DMA((2, num_heads, 2 * nrecv)),
            pltpu.SemaphoreType.DMA((4, num_heads, ne)),
            pltpu.SemaphoreType.DMA((4, num_heads, ne)),
            pltpu.SemaphoreType.DMA((4, num_heads)),
        ],
        compiler_params=pltpu.CompilerParams(
            collective_id=0, has_side_effects=True, vmem_limit_bytes=56 * 1024 * 1024
        ),
    )(weights, scalars, query_tok, key_tok, value_tok, grad_out)


def solution(mesh):
    placed = (P("seq", "exp"), P("seq", "exp"), P("seq", "exp"), P("seq", "exp"), P("exp"))
    return jax.shard_map(
        shards,
        mesh=mesh,
        in_specs=placed,
        out_specs=(
            P(("seq", "exp"), None),
            P(("seq", "exp"), None),
            P(("seq", "exp"), None),
            P(("seq", "exp"), None),
        ),
        check_vma=False,
    )
```

```python
import functools

import jax
import jax.numpy as jnp
from jax import lax
from jax.experimental import pallas as pl
from jax.experimental.pallas import tpu as pltpu
from jax.sharding import PartitionSpec as P


MESH = pl.DeviceIdType.MESH


def whole_kernel(n, near, far, w_ref, scal_ref, q_ref, k_ref, v_ref, do_ref,
                 o0, o1, o2, o3, dk_ref, dq_ref, kx, qx, krecv, qrecv, s_acc, r_acc, intra, stage, wts, gwts,
                 scan_sems, send_sems, recv_sems, local_sems):
    outs = (o0, o1, o2, o3)
    me_s = lax.axis_index("seq")
    me = lax.axis_index("exp")
    ne = lax.axis_size("exp")
    length, width = q_ref.shape
    heads = scal_ref.shape[0] // 2
    hd = width // heads
    slab = length // ne
    blk = min(256, length)
    nblk = length // blk
    hi = lax.Precision.HIGHEST
    f32 = jnp.float32
    nt = (((1,), (1,)), ((), ()))
    tn = (((0,), (0,)), ((), ()))

    def cols(h):
        return pl.ds(h * hd, hd)

    place = lax.broadcasted_iota(jnp.int32, (length, 1), 0).astype(f32)
    for h in range(heads):
        rate = scal_ref[h]
        keyed = (k_ref[:, cols(h)].astype(f32) * jnp.exp(-rate * (length - place))).astype(jnp.bfloat16)
        dk_ref[h] = lax.dot_general(keyed, v_ref[:, cols(h)], tn, preferred_element_type=f32)
        queried = (q_ref[:, cols(h)].astype(f32) * jnp.exp(-rate * (place + 1.0))).astype(jnp.bfloat16)
        dq_ref[h] = lax.dot_general(queried, do_ref[:, cols(h)], tn, preferred_element_type=f32)

    barrier = pltpu.get_barrier_semaphore()
    partners = sorted(set(near + [1, far]))
    peers = ne - 1
    for d in partners:
        for other in (me_s + d, me_s - d):
            @pl.when(jnp.logical_and(other >= 0, other < n))
            def _():
                pl.semaphore_signal(barrier, 1, device_id=(other, me), device_id_type=MESH)
            peers = peers + jnp.logical_and(other >= 0, other < n).astype(jnp.int32)
    for j in range(1, ne):
        pl.semaphore_signal(barrier, 1, device_id=(me_s, lax.rem(me + j, ne)), device_id_type=MESH)
    pl.semaphore_wait(barrier, peers)

    def weights_task(h):
        def run():
            rate = scal_ref[h]
            scale = scal_ref[heads + h]
            qh = q_ref[:, cols(h)]
            kh = k_ref[:, cols(h)]
            vh = v_ref[:, cols(h)]
            dh = do_ref[:, cols(h)]
            for b in range(nblk):
                rows = pl.ds(b * blk, blk)
                i = (lax.broadcasted_iota(jnp.int32, (blk, length), 0) + b * blk).astype(f32)
                jj = lax.broadcasted_iota(jnp.int32, (blk, length), 1).astype(f32)
                off = i - jj
                damp = jnp.where(off >= 0, jnp.exp(-rate * jnp.maximum(off, 0.0)), 0.0) * scale
                sc = lax.dot_general(qh[b * blk:(b + 1) * blk], kh, nt, preferred_element_type=f32)
                wts[h, rows, :] = (sc * damp).astype(jnp.bfloat16)
                gs = lax.dot_general(dh[b * blk:(b + 1) * blk], vh, nt, preferred_element_type=f32)
                gwts[h, rows, :] = (gs * damp).astype(jnp.bfloat16)
        return run

    def intra_task(h, o):
        def run():
            for b in range(nblk):
                rows = pl.ds(b * blk, blk)
                if o == 0:
                    res = jnp.dot(wts[h, rows, :], v_ref[:, cols(h)], preferred_element_type=f32)
                elif o == 1:
                    res = jnp.dot(gwts[h, rows, :], k_ref[:, cols(h)], preferred_element_type=f32)
                elif o == 2:
                    res = lax.dot_general(gwts[h, :, rows], q_ref[:, cols(h)], tn, preferred_element_type=f32)
                else:
                    res = lax.dot_general(wts[h, :, rows], do_ref[:, cols(h)], tn, preferred_element_type=f32)
                intra[o, rows, cols(h)] = res
        return run

    def copy(src, dst, h, slot, other):
        return pltpu.make_async_remote_copy(
            src_ref=src, dst_ref=dst, send_sem=scan_sems.at[0, h, slot], recv_sem=scan_sems.at[1, h, slot],
            device_id=(lax.rem(other + n, n), me), device_id_type=MESH,
        )

    order = []
    for j in range(1, ne):
        for cand in (j, ne - j):
            if 0 < cand < ne and cand not in order:
                order.append(cand)

    def send(o, h):
        for j in order:
            peer = lax.rem(me + j, ne)
            pltpu.make_async_remote_copy(
                src_ref=stage.at[o, pl.ds(pl.multiple_of(peer * slab, slab), slab), cols(h)],
                dst_ref=outs[o].at[:, pl.ds(pl.multiple_of(me * width + h * hd, hd), hd)],
                send_sem=send_sems.at[o, h, j], recv_sem=recv_sems.at[o, h, j],
                device_id=(me_s, peer), device_id_type=MESH,
            ).start()
        pltpu.make_async_copy(
            stage.at[o, pl.ds(pl.multiple_of(me * slab, slab), slab), cols(h)],
            outs[o].at[:, pl.ds(pl.multiple_of(me * width + h * hd, hd), hd)],
            local_sems.at[o, h],
        ).start()

    def pos(b):
        return (lax.broadcasted_iota(jnp.int32, (blk, 1), 0) + b * blk).astype(f32)

    nround = len(near) + 1
    sent = []
    last = len(near)
    pending = []

    def flush_one():
        if pending:
            pending.pop(0)()

    for h in range(heads):
        mine = [weights_task(h)] + [intra_task(h, o) for o in range(4)]
        per_round = -(-len(mine) // nround)
        kcur, qcur = dk_ref.at[h], dq_ref.at[h]
        for r, d in enumerate(near):
            kc = copy(kcur, krecv.at[r, h], h, 2 * r, me_s + d)
            qc = copy(qcur, qrecv.at[r, h], h, 2 * r + 1, me_s - d)
            pl.when(me_s + d < n)(kc.start)
            pl.when(me_s - d >= 0)(qc.start)
            sent.append((kc, me_s + d < n))
            sent.append((qc, me_s - d >= 0))
            flush_one()
            for task in mine[r * per_round:(r + 1) * per_round]:
                task()
            for cur, nxt, recv, cp, has in ((kcur, kx, krecv, kc, me_s - d >= 0), (qcur, qx, qrecv, qc, me_s + d < n)):
                @pl.when(has)
                def _():
                    cp.wait_recv()
                    nxt[r, h] = cur[...] + w_ref[r * heads + h] * recv[r, h]

                @pl.when(jnp.logical_not(has))
                def _():
                    nxt[r, h] = cur[...]
            kcur, qcur = kx.at[r, h], qx.at[r, h]
        finals = []
        for j, d in enumerate((1, far)):
            slot = 2 * (last + j)
            kc = copy(kcur, krecv.at[last + j, h], h, slot, me_s + d)
            qc = copy(qcur, qrecv.at[last + j, h], h, slot + 1, me_s - d)
            pl.when(me_s + d < n)(kc.start)
            pl.when(me_s - d >= 0)(qc.start)
            sent.append((kc, me_s + d < n))
            sent.append((qc, me_s - d >= 0))
            finals.append((kc, qc, d))
        flush_one()
        for task in mine[last * per_round:]:
            task()
        s_acc[h] = jnp.zeros((hd, hd), f32)
        r_acc[h] = jnp.zeros((hd, hd), f32)
        for j, (kc, qc, d) in enumerate(finals):
            for cp, recv, acc, has in ((kc, krecv, s_acc, me_s - d >= 0), (qc, qrecv, r_acc, me_s + d < n)):
                @pl.when(has)
                def _():
                    cp.wait_recv()
                    scale = 1.0 if j == 0 else w_ref[last * heads + h]
                    acc[h] = acc[h] + scale * recv[last + j, h]

        def stage_send(h, o):
            def run():
                rate = scal_ref[h]
                scale = scal_ref[heads + h]
                for b in range(nblk):
                    rows = pl.ds(b * blk, blk)
                    if o == 0:
                        lead = scale * jnp.exp(-rate * pos(b))
                        extra = lead * jnp.dot(q_ref[rows, cols(h)].astype(f32), s_acc[h], precision=hi, preferred_element_type=f32)
                    elif o == 1:
                        lead = scale * jnp.exp(-rate * pos(b))
                        extra = lead * lax.dot_general(do_ref[rows, cols(h)].astype(f32), s_acc[h], nt, precision=hi, preferred_element_type=f32)
                    elif o == 2:
                        trail = scale * jnp.exp(-rate * (length - 1.0 - pos(b)))
                        extra = trail * lax.dot_general(v_ref[rows, cols(h)].astype(f32), r_acc[h], nt, precision=hi, preferred_element_type=f32)
                    else:
                        trail = scale * jnp.exp(-rate * (length - 1.0 - pos(b)))
                        extra = trail * jnp.dot(k_ref[rows, cols(h)].astype(f32), r_acc[h], precision=hi, preferred_element_type=f32)
                    stage[o, rows, cols(h)] = (intra[o, rows, cols(h)] + extra).astype(jnp.bfloat16)
                send(o, h)
            return run

        batches = [stage_send(h, o) for o in range(4)]
        if h < heads - 1:
            batches[0]()
            pending.extend(batches[1:])
        else:
            while pending:
                flush_one()
            for run in batches:
                run()

    for cp, cond in sent:
        pl.when(cond)(cp.wait_send)
    for o in range(4):
        for h in range(heads):
            for j in range(1, ne):
                cp = pltpu.make_async_remote_copy(
                    src_ref=stage.at[o, pl.ds(0, slab), cols(h)],
                    dst_ref=outs[o].at[:, pl.ds(h * hd, hd)],
                    send_sem=send_sems.at[o, h, j], recv_sem=recv_sems.at[o, h, j],
                    device_id=(me_s, lax.rem(me + j, ne)), device_id_type=MESH,
                )
                cp.wait_send()
                cp.wait_recv()
            pltpu.make_async_copy(
                stage.at[o, pl.ds(0, slab), cols(h)], outs[o].at[:, pl.ds(h * hd, hd)], local_sems.at[o, h]
            ).wait()


def shards(query_tok, key_tok, value_tok, grad_out, decay_rate):
    seg_len = query_tok.shape[0]
    num_heads = decay_rate.shape[0]
    head_size = query_tok.shape[1] // num_heads
    ne = lax.axis_size("exp")
    total_len = seg_len * lax.axis_size("seq")
    scale_head = jnp.sqrt((2.0 * decay_rate + 2.0 / total_len) / head_size)
    rate_len = decay_rate * seg_len
    n = lax.axis_size("seq")
    near = []
    d = 1
    while 2 * d < n:
        near.append(d)
        d *= 2
    far = d + 1
    dists = jnp.asarray(near + [d], jnp.float32)
    weights = jnp.exp(-dists[:, None] * rate_len[None, :]).reshape(-1)
    nrecv = len(near) + 2
    scalars = jnp.concatenate([decay_rate, scale_head]).astype(jnp.float32)
    width = query_tok.shape[1]
    slab = seg_len // ne
    out = jax.ShapeDtypeStruct((slab, ne * width), jnp.bfloat16)
    smem = pl.BlockSpec(memory_space=pltpu.SMEM)
    vspec = pl.BlockSpec(memory_space=pltpu.VMEM)
    anyspec = pl.BlockSpec(memory_space=pl.ANY)
    st = (num_heads, head_size, head_size)
    return pl.pallas_call(
        functools.partial(whole_kernel, n, near, far),
        out_shape=(out, out, out, out),
        in_specs=[smem, smem] + [vspec] * 4,
        out_specs=(anyspec, anyspec, anyspec, anyspec),
        scratch_shapes=[
            pltpu.VMEM(st, jnp.float32),
            pltpu.VMEM(st, jnp.float32),
            pltpu.VMEM((len(near),) + st, jnp.float32),
            pltpu.VMEM((len(near),) + st, jnp.float32),
            pltpu.VMEM((nrecv,) + st, jnp.float32),
            pltpu.VMEM((nrecv,) + st, jnp.float32),
            pltpu.VMEM(st, jnp.float32),
            pltpu.VMEM(st, jnp.float32),
            pltpu.VMEM((4, seg_len, width), jnp.float32),
            pltpu.VMEM((4, seg_len, width), jnp.bfloat16),
            pltpu.VMEM((num_heads, seg_len, seg_len), jnp.bfloat16),
            pltpu.VMEM((num_heads, seg_len, seg_len), jnp.bfloat16),
            pltpu.SemaphoreType.DMA((2, num_heads, 2 * nrecv)),
            pltpu.SemaphoreType.DMA((4, num_heads, ne)),
            pltpu.SemaphoreType.DMA((4, num_heads, ne)),
            pltpu.SemaphoreType.DMA((4, num_heads)),
        ],
        compiler_params=pltpu.CompilerParams(
            collective_id=0, has_side_effects=True, vmem_limit_bytes=56 * 1024 * 1024
        ),
    )(weights, scalars, query_tok, key_tok, value_tok, grad_out)


def solution(mesh):
    placed = (P("seq", "exp"), P("seq", "exp"), P("seq", "exp"), P("seq", "exp"), P("exp"))
    return jax.shard_map(
        shards,
        mesh=mesh,
        in_specs=placed,
        out_specs=(
            P(("seq", "exp"), None),
            P(("seq", "exp"), None),
            P(("seq", "exp"), None),
            P(("seq", "exp"), None),
        ),
        check_vma=False,
    )
```

```python
import functools

import jax
import jax.numpy as jnp
from jax import lax
from jax.experimental import pallas as pl
from jax.experimental.pallas import tpu as pltpu
from jax.sharding import PartitionSpec as P


MESH = pl.DeviceIdType.MESH


def whole_kernel(n, near, far, packed, q_ref, k_ref, v_ref, do_ref,
                 o0, o1, o2, o3, dk_ref, dq_ref, kx, qx, krecv, qrecv, s_acc, r_acc, intra, stage, wts, gwts,
                 scan_sems, send_sems, recv_sems, local_sems):
    outs = (o0, o1, o2, o3)
    heads = dk_ref.shape[0]
    nw = (len(near) + 1) * heads
    w_ref = packed
    scal_ref = packed.at[pl.ds(nw, 2 * heads)]
    me_s = lax.axis_index("seq")
    me = lax.axis_index("exp")
    ne = lax.axis_size("exp")
    length, width = q_ref.shape
    hd = width // heads
    slab = length // ne
    blk = min(256, length)
    nblk = length // blk
    hi = lax.Precision.HIGHEST
    f32 = jnp.float32
    nt = (((1,), (1,)), ((), ()))
    tn = (((0,), (0,)), ((), ()))

    def cols(h):
        return pl.ds(h * hd, hd)

    place = lax.broadcasted_iota(jnp.int32, (length, 1), 0).astype(f32)
    for h in range(heads):
        rate = scal_ref[h]
        keyed = (k_ref[:, cols(h)].astype(f32) * jnp.exp(-rate * (length - place))).astype(jnp.bfloat16)
        dk_ref[h] = lax.dot_general(keyed, v_ref[:, cols(h)], tn, preferred_element_type=f32)
        queried = (q_ref[:, cols(h)].astype(f32) * jnp.exp(-rate * (place + 1.0))).astype(jnp.bfloat16)
        dq_ref[h] = lax.dot_general(queried, do_ref[:, cols(h)], tn, preferred_element_type=f32)

    barrier = pltpu.get_barrier_semaphore()
    partners = sorted(set(near + [1, far]))
    peers = ne - 1
    for d in partners:
        for other in (me_s + d, me_s - d):
            @pl.when(jnp.logical_and(other >= 0, other < n))
            def _():
                pl.semaphore_signal(barrier, 1, device_id=(other, me), device_id_type=MESH)
            peers = peers + jnp.logical_and(other >= 0, other < n).astype(jnp.int32)
    for j in range(1, ne):
        pl.semaphore_signal(barrier, 1, device_id=(me_s, lax.rem(me + j, ne)), device_id_type=MESH)
    pl.semaphore_wait(barrier, peers)

    def weights_task(h):
        def run():
            rate = scal_ref[h]
            scale = scal_ref[heads + h]
            qh = q_ref[:, cols(h)]
            kh = k_ref[:, cols(h)]
            vh = v_ref[:, cols(h)]
            dh = do_ref[:, cols(h)]
            for b in range(nblk):
                rows = pl.ds(b * blk, blk)
                i = (lax.broadcasted_iota(jnp.int32, (blk, length), 0) + b * blk).astype(f32)
                jj = lax.broadcasted_iota(jnp.int32, (blk, length), 1).astype(f32)
                off = i - jj
                damp = jnp.where(off >= 0, jnp.exp(-rate * jnp.maximum(off, 0.0)), 0.0) * scale
                sc = lax.dot_general(qh[b * blk:(b + 1) * blk], kh, nt, preferred_element_type=f32)
                wts[h, rows, :] = (sc * damp).astype(jnp.bfloat16)
                gs = lax.dot_general(dh[b * blk:(b + 1) * blk], vh, nt, preferred_element_type=f32)
                gwts[h, rows, :] = (gs * damp).astype(jnp.bfloat16)
        return run

    def intra_task(h, o):
        def run():
            for b in range(nblk):
                rows = pl.ds(b * blk, blk)
                if o == 0:
                    res = jnp.dot(wts[h, rows, :], v_ref[:, cols(h)], preferred_element_type=f32)
                elif o == 1:
                    res = jnp.dot(gwts[h, rows, :], k_ref[:, cols(h)], preferred_element_type=f32)
                elif o == 2:
                    res = lax.dot_general(gwts[h, :, rows], q_ref[:, cols(h)], tn, preferred_element_type=f32)
                else:
                    res = lax.dot_general(wts[h, :, rows], do_ref[:, cols(h)], tn, preferred_element_type=f32)
                intra[o, rows, cols(h)] = res
        return run

    def copy(src, dst, h, slot, other):
        return pltpu.make_async_remote_copy(
            src_ref=src, dst_ref=dst, send_sem=scan_sems.at[0, h, slot], recv_sem=scan_sems.at[1, h, slot],
            device_id=(lax.rem(other + n, n), me), device_id_type=MESH,
        )

    order = []
    for j in range(1, ne):
        for cand in (j, ne - j):
            if 0 < cand < ne and cand not in order:
                order.append(cand)

    def send(o, h):
        for j in order:
            peer = lax.rem(me + j, ne)
            pltpu.make_async_remote_copy(
                src_ref=stage.at[o, pl.ds(pl.multiple_of(peer * slab, slab), slab), cols(h)],
                dst_ref=outs[o].at[:, pl.ds(pl.multiple_of(me * width + h * hd, hd), hd)],
                send_sem=send_sems.at[o, h, j], recv_sem=recv_sems.at[o, h, j],
                device_id=(me_s, peer), device_id_type=MESH,
            ).start()
        pltpu.make_async_copy(
            stage.at[o, pl.ds(pl.multiple_of(me * slab, slab), slab), cols(h)],
            outs[o].at[:, pl.ds(pl.multiple_of(me * width + h * hd, hd), hd)],
            local_sems.at[o, h],
        ).start()

    def pos(b):
        return (lax.broadcasted_iota(jnp.int32, (blk, 1), 0) + b * blk).astype(f32)

    nround = len(near) + 1
    sent = []
    last = len(near)
    pending = []

    def flush_one():
        if pending:
            pending.pop(0)()

    for h in range(heads):
        mine = [weights_task(h)] + [intra_task(h, o) for o in range(4)]
        per_round = -(-len(mine) // nround)
        kcur, qcur = dk_ref.at[h], dq_ref.at[h]
        for r, d in enumerate(near):
            kc = copy(kcur, krecv.at[r, h], h, 2 * r, me_s + d)
            qc = copy(qcur, qrecv.at[r, h], h, 2 * r + 1, me_s - d)
            pl.when(me_s + d < n)(kc.start)
            pl.when(me_s - d >= 0)(qc.start)
            sent.append((kc, me_s + d < n))
            sent.append((qc, me_s - d >= 0))
            flush_one()
            for task in mine[r * per_round:(r + 1) * per_round]:
                task()
            for cur, nxt, recv, cp, has in ((kcur, kx, krecv, kc, me_s - d >= 0), (qcur, qx, qrecv, qc, me_s + d < n)):
                @pl.when(has)
                def _():
                    cp.wait_recv()
                    nxt[r, h] = cur[...] + w_ref[r * heads + h] * recv[r, h]

                @pl.when(jnp.logical_not(has))
                def _():
                    nxt[r, h] = cur[...]
            kcur, qcur = kx.at[r, h], qx.at[r, h]
        finals = []
        for j, d in enumerate((1, far)):
            slot = 2 * (last + j)
            kc = copy(kcur, krecv.at[last + j, h], h, slot, me_s + d)
            qc = copy(qcur, qrecv.at[last + j, h], h, slot + 1, me_s - d)
            pl.when(me_s + d < n)(kc.start)
            pl.when(me_s - d >= 0)(qc.start)
            sent.append((kc, me_s + d < n))
            sent.append((qc, me_s - d >= 0))
            finals.append((kc, qc, d))
        flush_one()
        for task in mine[last * per_round:]:
            task()
        s_acc[h] = jnp.zeros((hd, hd), f32)
        r_acc[h] = jnp.zeros((hd, hd), f32)
        for j, (kc, qc, d) in enumerate(finals):
            for cp, recv, acc, has in ((kc, krecv, s_acc, me_s - d >= 0), (qc, qrecv, r_acc, me_s + d < n)):
                @pl.when(has)
                def _():
                    cp.wait_recv()
                    scale = 1.0 if j == 0 else w_ref[last * heads + h]
                    acc[h] = acc[h] + scale * recv[last + j, h]

        def stage_send(h, o):
            def run():
                rate = scal_ref[h]
                scale = scal_ref[heads + h]
                for b in range(nblk):
                    rows = pl.ds(b * blk, blk)
                    if o == 0:
                        lead = scale * jnp.exp(-rate * pos(b))
                        extra = lead * jnp.dot(q_ref[rows, cols(h)].astype(f32), s_acc[h], precision=hi, preferred_element_type=f32)
                    elif o == 1:
                        lead = scale * jnp.exp(-rate * pos(b))
                        extra = lead * lax.dot_general(do_ref[rows, cols(h)].astype(f32), s_acc[h], nt, precision=hi, preferred_element_type=f32)
                    elif o == 2:
                        trail = scale * jnp.exp(-rate * (length - 1.0 - pos(b)))
                        extra = trail * lax.dot_general(v_ref[rows, cols(h)].astype(f32), r_acc[h], nt, precision=hi, preferred_element_type=f32)
                    else:
                        trail = scale * jnp.exp(-rate * (length - 1.0 - pos(b)))
                        extra = trail * jnp.dot(k_ref[rows, cols(h)].astype(f32), r_acc[h], precision=hi, preferred_element_type=f32)
                    stage[o, rows, cols(h)] = (intra[o, rows, cols(h)] + extra).astype(jnp.bfloat16)
                send(o, h)
            return run

        batches = [stage_send(h, o) for o in range(4)]
        if h < heads - 1:
            batches[0]()
            pending.extend(batches[1:])
        else:
            while pending:
                flush_one()
            for run in batches:
                run()

    for cp, cond in sent:
        pl.when(cond)(cp.wait_send)
    for o in range(4):
        for h in range(heads):
            for j in range(1, ne):
                cp = pltpu.make_async_remote_copy(
                    src_ref=stage.at[o, pl.ds(0, slab), cols(h)],
                    dst_ref=outs[o].at[:, pl.ds(h * hd, hd)],
                    send_sem=send_sems.at[o, h, j], recv_sem=recv_sems.at[o, h, j],
                    device_id=(me_s, lax.rem(me + j, ne)), device_id_type=MESH,
                )
                cp.wait_send()
                cp.wait_recv()
            pltpu.make_async_copy(
                stage.at[o, pl.ds(0, slab), cols(h)], outs[o].at[:, pl.ds(h * hd, hd)], local_sems.at[o, h]
            ).wait()


def shards(query_tok, key_tok, value_tok, grad_out, decay_rate):
    seg_len = query_tok.shape[0]
    num_heads = decay_rate.shape[0]
    head_size = query_tok.shape[1] // num_heads
    ne = lax.axis_size("exp")
    total_len = seg_len * lax.axis_size("seq")
    scale_head = jnp.sqrt((2.0 * decay_rate + 2.0 / total_len) / head_size)
    rate_len = decay_rate * seg_len
    n = lax.axis_size("seq")
    near = []
    d = 1
    while 2 * d < n:
        near.append(d)
        d *= 2
    far = d + 1
    dists = jnp.asarray(near + [d], jnp.float32)
    weights = jnp.exp(-dists[:, None] * rate_len[None, :]).reshape(-1)
    nrecv = len(near) + 2
    packed = jnp.concatenate([weights, decay_rate, scale_head]).astype(jnp.float32)
    width = query_tok.shape[1]
    slab = seg_len // ne
    out = jax.ShapeDtypeStruct((slab, ne * width), jnp.bfloat16)
    smem = pl.BlockSpec(memory_space=pltpu.SMEM)
    vspec = pl.BlockSpec(memory_space=pltpu.VMEM)
    anyspec = pl.BlockSpec(memory_space=pl.ANY)
    st = (num_heads, head_size, head_size)
    return pl.pallas_call(
        functools.partial(whole_kernel, n, near, far),
        out_shape=(out, out, out, out),
        in_specs=[smem] + [vspec] * 4,
        out_specs=(anyspec, anyspec, anyspec, anyspec),
        scratch_shapes=[
            pltpu.VMEM(st, jnp.float32),
            pltpu.VMEM(st, jnp.float32),
            pltpu.VMEM((len(near),) + st, jnp.float32),
            pltpu.VMEM((len(near),) + st, jnp.float32),
            pltpu.VMEM((nrecv,) + st, jnp.float32),
            pltpu.VMEM((nrecv,) + st, jnp.float32),
            pltpu.VMEM(st, jnp.float32),
            pltpu.VMEM(st, jnp.float32),
            pltpu.VMEM((4, seg_len, width), jnp.float32),
            pltpu.VMEM((4, seg_len, width), jnp.bfloat16),
            pltpu.VMEM((num_heads, seg_len, seg_len), jnp.bfloat16),
            pltpu.VMEM((num_heads, seg_len, seg_len), jnp.bfloat16),
            pltpu.SemaphoreType.DMA((2, num_heads, 2 * nrecv)),
            pltpu.SemaphoreType.DMA((4, num_heads, ne)),
            pltpu.SemaphoreType.DMA((4, num_heads, ne)),
            pltpu.SemaphoreType.DMA((4, num_heads)),
        ],
        compiler_params=pltpu.CompilerParams(
            collective_id=0, has_side_effects=True, vmem_limit_bytes=56 * 1024 * 1024
        ),
    )(packed, query_tok, key_tok, value_tok, grad_out)


def solution(mesh):
    placed = (P("seq", "exp"), P("seq", "exp"), P("seq", "exp"), P("seq", "exp"), P("exp"))
    return jax.shard_map(
        shards,
        mesh=mesh,
        in_specs=placed,
        out_specs=(
            P(("seq", "exp"), None),
            P(("seq", "exp"), None),
            P(("seq", "exp"), None),
            P(("seq", "exp"), None),
        ),
        check_vma=False,
    )
```

```python
import functools

import jax
import jax.numpy as jnp
from jax import lax
from jax.experimental import pallas as pl
from jax.experimental.pallas import tpu as pltpu
from jax.sharding import PartitionSpec as P


MESH = pl.DeviceIdType.MESH


def whole_kernel(n, near, far, packed, q_ref, k_ref, v_ref, do_ref,
                 o0, o1, o2, o3, dk_ref, dq_ref, kx, qx, krecv, qrecv, s_acc, r_acc, intra, stage, wts, gwts,
                 scan_sems, send_sems, recv_sems, local_sems):
    outs = (o0, o1, o2, o3)
    heads = dk_ref.shape[0]
    nw = (len(near) + 1) * heads
    w_ref = packed
    scal_ref = packed.at[pl.ds(nw, 2 * heads)]
    me_s = lax.axis_index("seq")
    me = lax.axis_index("exp")
    ne = lax.axis_size("exp")
    length, width = q_ref.shape
    hd = width // heads
    slab = length // ne
    blk = min(256, length)
    nblk = length // blk
    hi = lax.Precision.HIGHEST
    f32 = jnp.float32
    nt = (((1,), (1,)), ((), ()))
    tn = (((0,), (0,)), ((), ()))

    def cols(h):
        return pl.ds(h * hd, hd)

    place = lax.broadcasted_iota(jnp.int32, (length, 1), 0).astype(f32)
    for h in range(heads):
        rate = scal_ref[h]
        keyed = (k_ref[:, cols(h)].astype(f32) * jnp.exp(-rate * (length - place))).astype(jnp.bfloat16)
        dk_ref[h] = lax.dot_general(keyed, v_ref[:, cols(h)], tn, preferred_element_type=f32)
        queried = (q_ref[:, cols(h)].astype(f32) * jnp.exp(-rate * (place + 1.0))).astype(jnp.bfloat16)
        dq_ref[h] = lax.dot_general(queried, do_ref[:, cols(h)], tn, preferred_element_type=f32)

    barrier = pltpu.get_barrier_semaphore()
    partners = sorted(set(near + [1, far]))
    peers = ne - 1
    for d in partners:
        for other in (me_s + d, me_s - d):
            @pl.when(jnp.logical_and(other >= 0, other < n))
            def _():
                pl.semaphore_signal(barrier, 1, device_id=(other, me), device_id_type=MESH)
            peers = peers + jnp.logical_and(other >= 0, other < n).astype(jnp.int32)
    for j in range(1, ne):
        pl.semaphore_signal(barrier, 1, device_id=(me_s, lax.rem(me + j, ne)), device_id_type=MESH)
    pl.semaphore_wait(barrier, peers)

    def weights_task(h):
        def run():
            rate = scal_ref[h]
            scale = scal_ref[heads + h]
            qh = q_ref[:, cols(h)]
            kh = k_ref[:, cols(h)]
            vh = v_ref[:, cols(h)]
            dh = do_ref[:, cols(h)]
            for b in range(nblk):
                rows = pl.ds(b * blk, blk)
                i = (lax.broadcasted_iota(jnp.int32, (blk, length), 0) + b * blk).astype(f32)
                jj = lax.broadcasted_iota(jnp.int32, (blk, length), 1).astype(f32)
                off = i - jj
                damp = jnp.where(off >= 0, jnp.exp(-rate * jnp.maximum(off, 0.0)), 0.0) * scale
                sc = lax.dot_general(qh[b * blk:(b + 1) * blk], kh, nt, preferred_element_type=f32)
                wts[h, rows, :] = (sc * damp).astype(jnp.bfloat16)
                gs = lax.dot_general(dh[b * blk:(b + 1) * blk], vh, nt, preferred_element_type=f32)
                gwts[h, rows, :] = (gs * damp).astype(jnp.bfloat16)
        return run

    def intra_task(h, o):
        def run():
            for b in range(nblk):
                rows = pl.ds(b * blk, blk)
                if o == 0:
                    res = jnp.dot(wts[h, rows, :], v_ref[:, cols(h)], preferred_element_type=f32)
                elif o == 1:
                    res = jnp.dot(gwts[h, rows, :], k_ref[:, cols(h)], preferred_element_type=f32)
                elif o == 2:
                    res = lax.dot_general(gwts[h, :, rows], q_ref[:, cols(h)], tn, preferred_element_type=f32)
                else:
                    res = lax.dot_general(wts[h, :, rows], do_ref[:, cols(h)], tn, preferred_element_type=f32)
                intra[o, rows, cols(h)] = res
        return run

    def copy(src, dst, h, slot, other):
        return pltpu.make_async_remote_copy(
            src_ref=src, dst_ref=dst, send_sem=scan_sems.at[0, h, slot], recv_sem=scan_sems.at[1, h, slot],
            device_id=(lax.rem(other + n, n), me), device_id_type=MESH,
        )

    order = []
    for j in range(1, ne):
        for cand in (j, ne - j):
            if 0 < cand < ne and cand not in order:
                order.append(cand)

    def send(o, h):
        for j in order:
            peer = lax.rem(me + j, ne)
            pltpu.make_async_remote_copy(
                src_ref=stage.at[o, pl.ds(pl.multiple_of(peer * slab, slab), slab), cols(h)],
                dst_ref=outs[o].at[:, pl.ds(pl.multiple_of(me * width + h * hd, hd), hd)],
                send_sem=send_sems.at[o, h, j], recv_sem=recv_sems.at[o, h, j],
                device_id=(me_s, peer), device_id_type=MESH,
            ).start()
        pltpu.make_async_copy(
            stage.at[o, pl.ds(pl.multiple_of(me * slab, slab), slab), cols(h)],
            outs[o].at[:, pl.ds(pl.multiple_of(me * width + h * hd, hd), hd)],
            local_sems.at[o, h],
        ).start()

    def pos(b):
        return (lax.broadcasted_iota(jnp.int32, (blk, 1), 0) + b * blk).astype(f32)

    nround = len(near) + 1
    sent = []
    last = len(near)
    pending = []

    def flush_one():
        if pending:
            pending.pop(0)()

    early = {}

    def first_round(h):
        d = near[0]
        kc = copy(dk_ref.at[h], krecv.at[0, h], h, 0, me_s + d)
        qc = copy(dq_ref.at[h], qrecv.at[0, h], h, 1, me_s - d)
        pl.when(me_s + d < n)(kc.start)
        pl.when(me_s - d >= 0)(qc.start)
        sent.append((kc, me_s + d < n))
        sent.append((qc, me_s - d >= 0))
        return kc, qc

    for h in range(heads):
        mine = [weights_task(h)] + [intra_task(h, o) for o in range(4)]
        per_round = -(-len(mine) // nround)
        kcur, qcur = dk_ref.at[h], dq_ref.at[h]
        for r, d in enumerate(near):
            if r == 0:
                kc, qc = early.pop(h) if h in early else first_round(h)
            else:
                kc = copy(kcur, krecv.at[r, h], h, 2 * r, me_s + d)
                qc = copy(qcur, qrecv.at[r, h], h, 2 * r + 1, me_s - d)
                pl.when(me_s + d < n)(kc.start)
                pl.when(me_s - d >= 0)(qc.start)
                sent.append((kc, me_s + d < n))
                sent.append((qc, me_s - d >= 0))
            flush_one()
            for task in mine[r * per_round:(r + 1) * per_round]:
                task()
            for cur, nxt, recv, cp, has in ((kcur, kx, krecv, kc, me_s - d >= 0), (qcur, qx, qrecv, qc, me_s + d < n)):
                @pl.when(has)
                def _():
                    cp.wait_recv()
                    nxt[r, h] = cur[...] + w_ref[r * heads + h] * recv[r, h]

                @pl.when(jnp.logical_not(has))
                def _():
                    nxt[r, h] = cur[...]
            kcur, qcur = kx.at[r, h], qx.at[r, h]
        finals = []
        for j, d in enumerate((1, far)):
            slot = 2 * (last + j)
            kc = copy(kcur, krecv.at[last + j, h], h, slot, me_s + d)
            qc = copy(qcur, qrecv.at[last + j, h], h, slot + 1, me_s - d)
            pl.when(me_s + d < n)(kc.start)
            pl.when(me_s - d >= 0)(qc.start)
            sent.append((kc, me_s + d < n))
            sent.append((qc, me_s - d >= 0))
            finals.append((kc, qc, d))
        if near and h + 1 < heads:
            early[h + 1] = first_round(h + 1)
        flush_one()
        for task in mine[last * per_round:]:
            task()
        s_acc[h] = jnp.zeros((hd, hd), f32)
        r_acc[h] = jnp.zeros((hd, hd), f32)
        for j, (kc, qc, d) in enumerate(finals):
            for cp, recv, acc, has in ((kc, krecv, s_acc, me_s - d >= 0), (qc, qrecv, r_acc, me_s + d < n)):
                @pl.when(has)
                def _():
                    cp.wait_recv()
                    scale = 1.0 if j == 0 else w_ref[last * heads + h]
                    acc[h] = acc[h] + scale * recv[last + j, h]

        def stage_send(h, o):
            def run():
                rate = scal_ref[h]
                scale = scal_ref[heads + h]
                for b in range(nblk):
                    rows = pl.ds(b * blk, blk)
                    if o == 0:
                        lead = scale * jnp.exp(-rate * pos(b))
                        extra = lead * jnp.dot(q_ref[rows, cols(h)].astype(f32), s_acc[h], precision=hi, preferred_element_type=f32)
                    elif o == 1:
                        lead = scale * jnp.exp(-rate * pos(b))
                        extra = lead * lax.dot_general(do_ref[rows, cols(h)].astype(f32), s_acc[h], nt, precision=hi, preferred_element_type=f32)
                    elif o == 2:
                        trail = scale * jnp.exp(-rate * (length - 1.0 - pos(b)))
                        extra = trail * lax.dot_general(v_ref[rows, cols(h)].astype(f32), r_acc[h], nt, precision=hi, preferred_element_type=f32)
                    else:
                        trail = scale * jnp.exp(-rate * (length - 1.0 - pos(b)))
                        extra = trail * jnp.dot(k_ref[rows, cols(h)].astype(f32), r_acc[h], precision=hi, preferred_element_type=f32)
                    stage[o, rows, cols(h)] = (intra[o, rows, cols(h)] + extra).astype(jnp.bfloat16)
                send(o, h)
            return run

        batches = [stage_send(h, o) for o in range(4)]
        if h < heads - 1:
            batches[0]()
            pending.extend(batches[1:])
        else:
            while pending:
                flush_one()
            for run in batches:
                run()

    for cp, cond in sent:
        pl.when(cond)(cp.wait_send)
    for o in range(4):
        for h in range(heads):
            for j in range(1, ne):
                cp = pltpu.make_async_remote_copy(
                    src_ref=stage.at[o, pl.ds(0, slab), cols(h)],
                    dst_ref=outs[o].at[:, pl.ds(h * hd, hd)],
                    send_sem=send_sems.at[o, h, j], recv_sem=recv_sems.at[o, h, j],
                    device_id=(me_s, lax.rem(me + j, ne)), device_id_type=MESH,
                )
                cp.wait_send()
                cp.wait_recv()
            pltpu.make_async_copy(
                stage.at[o, pl.ds(0, slab), cols(h)], outs[o].at[:, pl.ds(h * hd, hd)], local_sems.at[o, h]
            ).wait()


def shards(query_tok, key_tok, value_tok, grad_out, decay_rate):
    seg_len = query_tok.shape[0]
    num_heads = decay_rate.shape[0]
    head_size = query_tok.shape[1] // num_heads
    ne = lax.axis_size("exp")
    total_len = seg_len * lax.axis_size("seq")
    scale_head = jnp.sqrt((2.0 * decay_rate + 2.0 / total_len) / head_size)
    rate_len = decay_rate * seg_len
    n = lax.axis_size("seq")
    near = []
    d = 1
    while 2 * d < n:
        near.append(d)
        d *= 2
    far = d + 1
    dists = jnp.asarray(near + [d], jnp.float32)
    weights = jnp.exp(-dists[:, None] * rate_len[None, :]).reshape(-1)
    nrecv = len(near) + 2
    packed = jnp.concatenate([weights, decay_rate, scale_head]).astype(jnp.float32)
    width = query_tok.shape[1]
    slab = seg_len // ne
    out = jax.ShapeDtypeStruct((slab, ne * width), jnp.bfloat16)
    smem = pl.BlockSpec(memory_space=pltpu.SMEM)
    vspec = pl.BlockSpec(memory_space=pltpu.VMEM)
    anyspec = pl.BlockSpec(memory_space=pl.ANY)
    st = (num_heads, head_size, head_size)
    return pl.pallas_call(
        functools.partial(whole_kernel, n, near, far),
        out_shape=(out, out, out, out),
        in_specs=[smem] + [vspec] * 4,
        out_specs=(anyspec, anyspec, anyspec, anyspec),
        scratch_shapes=[
            pltpu.VMEM(st, jnp.float32),
            pltpu.VMEM(st, jnp.float32),
            pltpu.VMEM((len(near),) + st, jnp.float32),
            pltpu.VMEM((len(near),) + st, jnp.float32),
            pltpu.VMEM((nrecv,) + st, jnp.float32),
            pltpu.VMEM((nrecv,) + st, jnp.float32),
            pltpu.VMEM(st, jnp.float32),
            pltpu.VMEM(st, jnp.float32),
            pltpu.VMEM((4, seg_len, width), jnp.float32),
            pltpu.VMEM((4, seg_len, width), jnp.bfloat16),
            pltpu.VMEM((num_heads, seg_len, seg_len), jnp.bfloat16),
            pltpu.VMEM((num_heads, seg_len, seg_len), jnp.bfloat16),
            pltpu.SemaphoreType.DMA((2, num_heads, 2 * nrecv)),
            pltpu.SemaphoreType.DMA((4, num_heads, ne)),
            pltpu.SemaphoreType.DMA((4, num_heads, ne)),
            pltpu.SemaphoreType.DMA((4, num_heads)),
        ],
        compiler_params=pltpu.CompilerParams(
            collective_id=0, has_side_effects=True, vmem_limit_bytes=56 * 1024 * 1024
        ),
    )(packed, query_tok, key_tok, value_tok, grad_out)


def solution(mesh):
    placed = (P("seq", "exp"), P("seq", "exp"), P("seq", "exp"), P("seq", "exp"), P("exp"))
    return jax.shard_map(
        shards,
        mesh=mesh,
        in_specs=placed,
        out_specs=(
            P(("seq", "exp"), None),
            P(("seq", "exp"), None),
            P(("seq", "exp"), None),
            P(("seq", "exp"), None),
        ),
        check_vma=False,
    )
```

```python
import functools

import jax
import jax.numpy as jnp
from jax import lax
from jax.experimental import pallas as pl
from jax.experimental.pallas import tpu as pltpu
from jax.sharding import PartitionSpec as P


MESH = pl.DeviceIdType.MESH


def whole_kernel(n, near, far, packed, q_ref, k_ref, v_ref, do_ref,
                 o0, o1, o2, o3, dk_ref, dq_ref, kx, qx, krecv, qrecv, s_acc, r_acc, intra, stage, wts, gwts,
                 scan_sems, send_sems, recv_sems, local_sems):
    outs = (o0, o1, o2, o3)
    heads = dk_ref.shape[0]
    nw = (len(near) + 1) * heads
    w_ref = packed
    scal_ref = packed.at[pl.ds(nw, 2 * heads)]
    me_s = lax.axis_index("seq")
    me = lax.axis_index("exp")
    ne = lax.axis_size("exp")
    length, width = q_ref.shape
    hd = width // heads
    slab = length // ne
    blk = min(256, length)
    nblk = length // blk
    hi = lax.Precision.HIGHEST
    f32 = jnp.float32
    nt = (((1,), (1,)), ((), ()))
    tn = (((0,), (0,)), ((), ()))

    def cols(h):
        return pl.ds(h * hd, hd)

    place = lax.broadcasted_iota(jnp.int32, (length, 1), 0).astype(f32)
    for h in range(heads):
        rate = scal_ref[h]
        keyed = (k_ref[:, cols(h)].astype(f32) * jnp.exp(-rate * (length - place))).astype(jnp.bfloat16)
        dk_ref[h] = lax.dot_general(keyed, v_ref[:, cols(h)], tn, preferred_element_type=f32)
        queried = (q_ref[:, cols(h)].astype(f32) * jnp.exp(-rate * (place + 1.0))).astype(jnp.bfloat16)
        dq_ref[h] = lax.dot_general(queried, do_ref[:, cols(h)], tn, preferred_element_type=f32)

    barrier = pltpu.get_barrier_semaphore()
    partners = sorted(set(near + [1, far]))
    peers = ne - 1
    for d in partners:
        for other in (me_s + d, me_s - d):
            @pl.when(jnp.logical_and(other >= 0, other < n))
            def _():
                pl.semaphore_signal(barrier, 1, device_id=(other, me), device_id_type=MESH)
            peers = peers + jnp.logical_and(other >= 0, other < n).astype(jnp.int32)
    for j in range(1, ne):
        pl.semaphore_signal(barrier, 1, device_id=(me_s, lax.rem(me + j, ne)), device_id_type=MESH)
    pl.semaphore_wait(barrier, peers)

    def weights_task(h):
        def run():
            rate = scal_ref[h]
            scale = scal_ref[heads + h]
            qh = q_ref[:, cols(h)]
            kh = k_ref[:, cols(h)]
            vh = v_ref[:, cols(h)]
            dh = do_ref[:, cols(h)]
            for b in range(nblk):
                rows = pl.ds(b * blk, blk)
                i = (lax.broadcasted_iota(jnp.int32, (blk, length), 0) + b * blk).astype(f32)
                jj = lax.broadcasted_iota(jnp.int32, (blk, length), 1).astype(f32)
                off = i - jj
                damp = jnp.where(off >= 0, jnp.exp(-rate * jnp.maximum(off, 0.0)), 0.0) * scale
                sc = lax.dot_general(qh[b * blk:(b + 1) * blk], kh, nt, preferred_element_type=f32)
                wts[h, rows, :] = (sc * damp).astype(jnp.bfloat16)
                gs = lax.dot_general(dh[b * blk:(b + 1) * blk], vh, nt, preferred_element_type=f32)
                gwts[h, rows, :] = (gs * damp).astype(jnp.bfloat16)
        return run

    def intra_task(h, o):
        def run():
            for b in range(nblk):
                rows = pl.ds(b * blk, blk)
                if o == 0:
                    res = jnp.dot(wts[h, rows, :], v_ref[:, cols(h)], preferred_element_type=f32)
                elif o == 1:
                    res = jnp.dot(gwts[h, rows, :], k_ref[:, cols(h)], preferred_element_type=f32)
                elif o == 2:
                    res = lax.dot_general(gwts[h, :, rows], q_ref[:, cols(h)], tn, preferred_element_type=f32)
                else:
                    res = lax.dot_general(wts[h, :, rows], do_ref[:, cols(h)], tn, preferred_element_type=f32)
                intra[o, rows, cols(h)] = res
        return run

    def copy(src, dst, h, slot, other):
        return pltpu.make_async_remote_copy(
            src_ref=src, dst_ref=dst, send_sem=scan_sems.at[0, h, slot], recv_sem=scan_sems.at[1, h, slot],
            device_id=(lax.rem(other + n, n), me), device_id_type=MESH,
        )

    order = []
    for j in range(1, ne):
        for cand in (j, ne - j):
            if 0 < cand < ne and cand not in order:
                order.append(cand)

    def send(o, h):
        for j in order:
            peer = lax.rem(me + j, ne)
            pltpu.make_async_remote_copy(
                src_ref=stage.at[o, pl.ds(pl.multiple_of(peer * slab, slab), slab), cols(h)],
                dst_ref=outs[o].at[:, pl.ds(pl.multiple_of(me * width + h * hd, hd), hd)],
                send_sem=send_sems.at[o, h, j], recv_sem=recv_sems.at[o, h, j],
                device_id=(me_s, peer), device_id_type=MESH,
            ).start()
        pltpu.make_async_copy(
            stage.at[o, pl.ds(pl.multiple_of(me * slab, slab), slab), cols(h)],
            outs[o].at[:, pl.ds(pl.multiple_of(me * width + h * hd, hd), hd)],
            local_sems.at[o, h],
        ).start()

    def pos(b):
        return (lax.broadcasted_iota(jnp.int32, (blk, 1), 0) + b * blk).astype(f32)

    nround = len(near) + 1
    sent = []
    last = len(near)
    pending = []

    def flush_one():
        if pending:
            pending.pop(0)()

    early = {}

    def first_round(h):
        d = near[0]
        kc = copy(dk_ref.at[h], krecv.at[0, h], h, 0, me_s + d)
        qc = copy(dq_ref.at[h], qrecv.at[0, h], h, 1, me_s - d)
        pl.when(me_s + d < n)(kc.start)
        pl.when(me_s - d >= 0)(qc.start)
        sent.append((kc, me_s + d < n))
        sent.append((qc, me_s - d >= 0))
        return kc, qc

    for h in range(heads):
        later = 2 if h < heads - 1 else 4
        mine = [weights_task(h)] + [intra_task(h, o) for o in range(later)]
        per_round = -(-len(mine) // nround)
        kcur, qcur = dk_ref.at[h], dq_ref.at[h]
        for r, d in enumerate(near):
            if r == 0:
                kc, qc = early.pop(h) if h in early else first_round(h)
            else:
                kc = copy(kcur, krecv.at[r, h], h, 2 * r, me_s + d)
                qc = copy(qcur, qrecv.at[r, h], h, 2 * r + 1, me_s - d)
                pl.when(me_s + d < n)(kc.start)
                pl.when(me_s - d >= 0)(qc.start)
                sent.append((kc, me_s + d < n))
                sent.append((qc, me_s - d >= 0))
            flush_one()
            for task in mine[r * per_round:(r + 1) * per_round]:
                task()
            for cur, nxt, recv, cp, has in ((kcur, kx, krecv, kc, me_s - d >= 0), (qcur, qx, qrecv, qc, me_s + d < n)):
                @pl.when(has)
                def _():
                    cp.wait_recv()
                    nxt[r, h] = cur[...] + w_ref[r * heads + h] * recv[r, h]

                @pl.when(jnp.logical_not(has))
                def _():
                    nxt[r, h] = cur[...]
            kcur, qcur = kx.at[r, h], qx.at[r, h]
        finals = []
        for j, d in enumerate((1, far)):
            slot = 2 * (last + j)
            kc = copy(kcur, krecv.at[last + j, h], h, slot, me_s + d)
            qc = copy(qcur, qrecv.at[last + j, h], h, slot + 1, me_s - d)
            pl.when(me_s + d < n)(kc.start)
            pl.when(me_s - d >= 0)(qc.start)
            sent.append((kc, me_s + d < n))
            sent.append((qc, me_s - d >= 0))
            finals.append((kc, qc, d))
        if near and h + 1 < heads:
            early[h + 1] = first_round(h + 1)
        flush_one()
        for task in mine[last * per_round:]:
            task()
        s_acc[h] = jnp.zeros((hd, hd), f32)
        r_acc[h] = jnp.zeros((hd, hd), f32)
        for j, (kc, qc, d) in enumerate(finals):
            for cp, recv, acc, has in ((kc, krecv, s_acc, me_s - d >= 0), (qc, qrecv, r_acc, me_s + d < n)):
                @pl.when(has)
                def _():
                    cp.wait_recv()
                    scale = 1.0 if j == 0 else w_ref[last * heads + h]
                    acc[h] = acc[h] + scale * recv[last + j, h]

        def stage_send(h, o):
            def run():
                rate = scal_ref[h]
                scale = scal_ref[heads + h]
                for b in range(nblk):
                    rows = pl.ds(b * blk, blk)
                    if o == 0:
                        lead = scale * jnp.exp(-rate * pos(b))
                        extra = lead * jnp.dot(q_ref[rows, cols(h)].astype(f32), s_acc[h], precision=hi, preferred_element_type=f32)
                    elif o == 1:
                        lead = scale * jnp.exp(-rate * pos(b))
                        extra = lead * lax.dot_general(do_ref[rows, cols(h)].astype(f32), s_acc[h], nt, precision=hi, preferred_element_type=f32)
                    elif o == 2:
                        trail = scale * jnp.exp(-rate * (length - 1.0 - pos(b)))
                        extra = trail * lax.dot_general(v_ref[rows, cols(h)].astype(f32), r_acc[h], nt, precision=hi, preferred_element_type=f32)
                    else:
                        trail = scale * jnp.exp(-rate * (length - 1.0 - pos(b)))
                        extra = trail * jnp.dot(k_ref[rows, cols(h)].astype(f32), r_acc[h], precision=hi, preferred_element_type=f32)
                    stage[o, rows, cols(h)] = (intra[o, rows, cols(h)] + extra).astype(jnp.bfloat16)
                send(o, h)
            return run

        def both(first, second):
            def run():
                first()
                second()
            return run

        batches = [stage_send(h, o) if o < later else both(intra_task(h, o), stage_send(h, o)) for o in range(4)]
        if h < heads - 1:
            batches[0]()
            pending.extend(batches[1:])
        else:
            while pending:
                flush_one()
            for run in batches:
                run()

    for cp, cond in sent:
        pl.when(cond)(cp.wait_send)
    for o in range(4):
        for h in range(heads):
            for j in range(1, ne):
                cp = pltpu.make_async_remote_copy(
                    src_ref=stage.at[o, pl.ds(0, slab), cols(h)],
                    dst_ref=outs[o].at[:, pl.ds(h * hd, hd)],
                    send_sem=send_sems.at[o, h, j], recv_sem=recv_sems.at[o, h, j],
                    device_id=(me_s, lax.rem(me + j, ne)), device_id_type=MESH,
                )
                cp.wait_send()
                cp.wait_recv()
            pltpu.make_async_copy(
                stage.at[o, pl.ds(0, slab), cols(h)], outs[o].at[:, pl.ds(h * hd, hd)], local_sems.at[o, h]
            ).wait()


def shards(query_tok, key_tok, value_tok, grad_out, decay_rate):
    seg_len = query_tok.shape[0]
    num_heads = decay_rate.shape[0]
    head_size = query_tok.shape[1] // num_heads
    ne = lax.axis_size("exp")
    total_len = seg_len * lax.axis_size("seq")
    scale_head = jnp.sqrt((2.0 * decay_rate + 2.0 / total_len) / head_size)
    rate_len = decay_rate * seg_len
    n = lax.axis_size("seq")
    near = []
    d = 1
    while 2 * d < n:
        near.append(d)
        d *= 2
    far = d + 1
    dists = jnp.asarray(near + [d], jnp.float32)
    weights = jnp.exp(-dists[:, None] * rate_len[None, :]).reshape(-1)
    nrecv = len(near) + 2
    packed = jnp.concatenate([weights, decay_rate, scale_head]).astype(jnp.float32)
    width = query_tok.shape[1]
    slab = seg_len // ne
    out = jax.ShapeDtypeStruct((slab, ne * width), jnp.bfloat16)
    smem = pl.BlockSpec(memory_space=pltpu.SMEM)
    vspec = pl.BlockSpec(memory_space=pltpu.VMEM)
    anyspec = pl.BlockSpec(memory_space=pl.ANY)
    st = (num_heads, head_size, head_size)
    return pl.pallas_call(
        functools.partial(whole_kernel, n, near, far),
        out_shape=(out, out, out, out),
        in_specs=[smem] + [vspec] * 4,
        out_specs=(anyspec, anyspec, anyspec, anyspec),
        scratch_shapes=[
            pltpu.VMEM(st, jnp.float32),
            pltpu.VMEM(st, jnp.float32),
            pltpu.VMEM((len(near),) + st, jnp.float32),
            pltpu.VMEM((len(near),) + st, jnp.float32),
            pltpu.VMEM((nrecv,) + st, jnp.float32),
            pltpu.VMEM((nrecv,) + st, jnp.float32),
            pltpu.VMEM(st, jnp.float32),
            pltpu.VMEM(st, jnp.float32),
            pltpu.VMEM((4, seg_len, width), jnp.float32),
            pltpu.VMEM((4, seg_len, width), jnp.bfloat16),
            pltpu.VMEM((num_heads, seg_len, seg_len), jnp.bfloat16),
            pltpu.VMEM((num_heads, seg_len, seg_len), jnp.bfloat16),
            pltpu.SemaphoreType.DMA((2, num_heads, 2 * nrecv)),
            pltpu.SemaphoreType.DMA((4, num_heads, ne)),
            pltpu.SemaphoreType.DMA((4, num_heads, ne)),
            pltpu.SemaphoreType.DMA((4, num_heads)),
        ],
        compiler_params=pltpu.CompilerParams(
            collective_id=0, has_side_effects=True, vmem_limit_bytes=56 * 1024 * 1024
        ),
    )(packed, query_tok, key_tok, value_tok, grad_out)


def solution(mesh):
    placed = (P("seq", "exp"), P("seq", "exp"), P("seq", "exp"), P("seq", "exp"), P("exp"))
    return jax.shard_map(
        shards,
        mesh=mesh,
        in_specs=placed,
        out_specs=(
            P(("seq", "exp"), None),
            P(("seq", "exp"), None),
            P(("seq", "exp"), None),
            P(("seq", "exp"), None),
        ),
        check_vma=False,
    )
```

```python
import functools

import jax
import jax.numpy as jnp
from jax import lax
from jax.experimental import pallas as pl
from jax.experimental.pallas import tpu as pltpu
from jax.sharding import PartitionSpec as P


MESH = pl.DeviceIdType.MESH


def whole_kernel(n, near, far, top, total, dec_ref, q_ref, k_ref, v_ref, do_ref,
                 o0, o1, o2, o3, dk_ref, dq_ref, kx, qx, krecv, qrecv, s_acc, r_acc, intra, stage, wts, gwts,
                 scan_sems, send_sems, recv_sems, local_sems):
    outs = (o0, o1, o2, o3)
    me_s = lax.axis_index("seq")
    me = lax.axis_index("exp")
    ne = lax.axis_size("exp")
    length, width = q_ref.shape
    heads = dec_ref.shape[0]
    hd = width // heads
    slab = length // ne
    blk = min(256, length)
    nblk = length // blk
    hi = lax.Precision.HIGHEST
    f32 = jnp.float32
    nt = (((1,), (1,)), ((), ()))
    tn = (((0,), (0,)), ((), ()))

    def cols(h):
        return pl.ds(h * hd, hd)

    rates = [jnp.full((1, 1), dec_ref[h], f32) for h in range(heads)]
    scales = [jnp.sqrt((2.0 * rates[h] + 2.0 / total) / hd) for h in range(heads)]
    wv = [[jnp.exp(-float(d) * (rates[h] * float(length))) for h in range(heads)] for d in near + [top]]
    place = lax.broadcasted_iota(jnp.int32, (length, 1), 0).astype(f32)
    for h in range(heads):
        rate = rates[h]
        keyed = (k_ref[:, cols(h)].astype(f32) * jnp.exp(-rate * (length - place))).astype(jnp.bfloat16)
        dk_ref[h] = lax.dot_general(keyed, v_ref[:, cols(h)], tn, preferred_element_type=f32)
        queried = (q_ref[:, cols(h)].astype(f32) * jnp.exp(-rate * (place + 1.0))).astype(jnp.bfloat16)
        dq_ref[h] = lax.dot_general(queried, do_ref[:, cols(h)], tn, preferred_element_type=f32)

    barrier = pltpu.get_barrier_semaphore()
    partners = sorted(set(near + [1, far]))
    peers = ne - 1
    for d in partners:
        for other in (me_s + d, me_s - d):
            @pl.when(jnp.logical_and(other >= 0, other < n))
            def _():
                pl.semaphore_signal(barrier, 1, device_id=(other, me), device_id_type=MESH)
            peers = peers + jnp.logical_and(other >= 0, other < n).astype(jnp.int32)
    for j in range(1, ne):
        pl.semaphore_signal(barrier, 1, device_id=(me_s, lax.rem(me + j, ne)), device_id_type=MESH)
    pl.semaphore_wait(barrier, peers)

    def weights_task(h):
        def run():
            rate = rates[h]
            scale = scales[h]
            qh = q_ref[:, cols(h)]
            kh = k_ref[:, cols(h)]
            vh = v_ref[:, cols(h)]
            dh = do_ref[:, cols(h)]
            for b in range(nblk):
                rows = pl.ds(b * blk, blk)
                i = (lax.broadcasted_iota(jnp.int32, (blk, length), 0) + b * blk).astype(f32)
                jj = lax.broadcasted_iota(jnp.int32, (blk, length), 1).astype(f32)
                off = i - jj
                damp = jnp.where(off >= 0, jnp.exp(-rate * jnp.maximum(off, 0.0)), 0.0) * scale
                sc = lax.dot_general(qh[b * blk:(b + 1) * blk], kh, nt, preferred_element_type=f32)
                wts[h, rows, :] = (sc * damp).astype(jnp.bfloat16)
                gs = lax.dot_general(dh[b * blk:(b + 1) * blk], vh, nt, preferred_element_type=f32)
                gwts[h, rows, :] = (gs * damp).astype(jnp.bfloat16)
        return run

    def intra_task(h, o):
        def run():
            for b in range(nblk):
                rows = pl.ds(b * blk, blk)
                if o == 0:
                    res = jnp.dot(wts[h, rows, :], v_ref[:, cols(h)], preferred_element_type=f32)
                elif o == 1:
                    res = jnp.dot(gwts[h, rows, :], k_ref[:, cols(h)], preferred_element_type=f32)
                elif o == 2:
                    res = lax.dot_general(gwts[h, :, rows], q_ref[:, cols(h)], tn, preferred_element_type=f32)
                else:
                    res = lax.dot_general(wts[h, :, rows], do_ref[:, cols(h)], tn, preferred_element_type=f32)
                intra[o, rows, cols(h)] = res
        return run

    def copy(src, dst, h, slot, other):
        return pltpu.make_async_remote_copy(
            src_ref=src, dst_ref=dst, send_sem=scan_sems.at[0, h, slot], recv_sem=scan_sems.at[1, h, slot],
            device_id=(lax.rem(other + n, n), me), device_id_type=MESH,
        )

    order = []
    for j in range(1, ne):
        for cand in (j, ne - j):
            if 0 < cand < ne and cand not in order:
                order.append(cand)

    def send(o, h):
        for j in order:
            peer = lax.rem(me + j, ne)
            pltpu.make_async_remote_copy(
                src_ref=stage.at[o, pl.ds(pl.multiple_of(peer * slab, slab), slab), cols(h)],
                dst_ref=outs[o].at[:, pl.ds(pl.multiple_of(me * width + h * hd, hd), hd)],
                send_sem=send_sems.at[o, h, j], recv_sem=recv_sems.at[o, h, j],
                device_id=(me_s, peer), device_id_type=MESH,
            ).start()
        pltpu.make_async_copy(
            stage.at[o, pl.ds(pl.multiple_of(me * slab, slab), slab), cols(h)],
            outs[o].at[:, pl.ds(pl.multiple_of(me * width + h * hd, hd), hd)],
            local_sems.at[o, h],
        ).start()

    def pos(b):
        return (lax.broadcasted_iota(jnp.int32, (blk, 1), 0) + b * blk).astype(f32)

    nround = len(near) + 1
    sent = []
    last = len(near)
    pending = []

    def flush_one():
        if pending:
            pending.pop(0)()

    for h in range(heads):
        mine = [weights_task(h)] + [intra_task(h, o) for o in range(4)]
        per_round = -(-len(mine) // nround)
        kcur, qcur = dk_ref.at[h], dq_ref.at[h]
        for r, d in enumerate(near):
            kc = copy(kcur, krecv.at[r, h], h, 2 * r, me_s + d)
            qc = copy(qcur, qrecv.at[r, h], h, 2 * r + 1, me_s - d)
            pl.when(me_s + d < n)(kc.start)
            pl.when(me_s - d >= 0)(qc.start)
            sent.append((kc, me_s + d < n))
            sent.append((qc, me_s - d >= 0))
            flush_one()
            for task in mine[r * per_round:(r + 1) * per_round]:
                task()
            for cur, nxt, recv, cp, has in ((kcur, kx, krecv, kc, me_s - d >= 0), (qcur, qx, qrecv, qc, me_s + d < n)):
                @pl.when(has)
                def _():
                    cp.wait_recv()
                    nxt[r, h] = cur[...] + wv[r][h] * recv[r, h]

                @pl.when(jnp.logical_not(has))
                def _():
                    nxt[r, h] = cur[...]
            kcur, qcur = kx.at[r, h], qx.at[r, h]
        finals = []
        for j, d in enumerate((1, far)):
            slot = 2 * (last + j)
            kc = copy(kcur, krecv.at[last + j, h], h, slot, me_s + d)
            qc = copy(qcur, qrecv.at[last + j, h], h, slot + 1, me_s - d)
            pl.when(me_s + d < n)(kc.start)
            pl.when(me_s - d >= 0)(qc.start)
            sent.append((kc, me_s + d < n))
            sent.append((qc, me_s - d >= 0))
            finals.append((kc, qc, d))
        flush_one()
        for task in mine[last * per_round:]:
            task()
        s_acc[h] = jnp.zeros((hd, hd), f32)
        r_acc[h] = jnp.zeros((hd, hd), f32)
        for j, (kc, qc, d) in enumerate(finals):
            for cp, recv, acc, has in ((kc, krecv, s_acc, me_s - d >= 0), (qc, qrecv, r_acc, me_s + d < n)):
                @pl.when(has)
                def _():
                    cp.wait_recv()
                    scale = 1.0 if j == 0 else wv[last][h]
                    acc[h] = acc[h] + scale * recv[last + j, h]

        def stage_send(h, o):
            def run():
                rate = rates[h]
                scale = scales[h]
                for b in range(nblk):
                    rows = pl.ds(b * blk, blk)
                    if o == 0:
                        lead = scale * jnp.exp(-rate * pos(b))
                        extra = lead * jnp.dot(q_ref[rows, cols(h)].astype(f32), s_acc[h], precision=hi, preferred_element_type=f32)
                    elif o == 1:
                        lead = scale * jnp.exp(-rate * pos(b))
                        extra = lead * lax.dot_general(do_ref[rows, cols(h)].astype(f32), s_acc[h], nt, precision=hi, preferred_element_type=f32)
                    elif o == 2:
                        trail = scale * jnp.exp(-rate * (length - 1.0 - pos(b)))
                        extra = trail * lax.dot_general(v_ref[rows, cols(h)].astype(f32), r_acc[h], nt, precision=hi, preferred_element_type=f32)
                    else:
                        trail = scale * jnp.exp(-rate * (length - 1.0 - pos(b)))
                        extra = trail * jnp.dot(k_ref[rows, cols(h)].astype(f32), r_acc[h], precision=hi, preferred_element_type=f32)
                    stage[o, rows, cols(h)] = (intra[o, rows, cols(h)] + extra).astype(jnp.bfloat16)
                send(o, h)
            return run

        batches = [stage_send(h, o) for o in range(4)]
        if h < heads - 1:
            batches[0]()
            pending.extend(batches[1:])
        else:
            while pending:
                flush_one()
            for run in batches:
                run()

    for cp, cond in sent:
        pl.when(cond)(cp.wait_send)
    for o in range(4):
        for h in range(heads):
            for j in range(1, ne):
                cp = pltpu.make_async_remote_copy(
                    src_ref=stage.at[o, pl.ds(0, slab), cols(h)],
                    dst_ref=outs[o].at[:, pl.ds(h * hd, hd)],
                    send_sem=send_sems.at[o, h, j], recv_sem=recv_sems.at[o, h, j],
                    device_id=(me_s, lax.rem(me + j, ne)), device_id_type=MESH,
                )
                cp.wait_send()
                cp.wait_recv()
            pltpu.make_async_copy(
                stage.at[o, pl.ds(0, slab), cols(h)], outs[o].at[:, pl.ds(h * hd, hd)], local_sems.at[o, h]
            ).wait()


def shards(query_tok, key_tok, value_tok, grad_out, decay_rate):
    seg_len = query_tok.shape[0]
    num_heads = decay_rate.shape[0]
    head_size = query_tok.shape[1] // num_heads
    ne = lax.axis_size("exp")
    total_len = seg_len * lax.axis_size("seq")
    n = lax.axis_size("seq")
    near = []
    d = 1
    while 2 * d < n:
        near.append(d)
        d *= 2
    far = d + 1
    nrecv = len(near) + 2
    width = query_tok.shape[1]
    slab = seg_len // ne
    out = jax.ShapeDtypeStruct((slab, ne * width), jnp.bfloat16)
    smem = pl.BlockSpec(memory_space=pltpu.SMEM)
    vspec = pl.BlockSpec(memory_space=pltpu.VMEM)
    anyspec = pl.BlockSpec(memory_space=pl.ANY)
    st = (num_heads, head_size, head_size)
    return pl.pallas_call(
        functools.partial(whole_kernel, n, near, far, d, total_len),
        out_shape=(out, out, out, out),
        in_specs=[smem] + [vspec] * 4,
        out_specs=(anyspec, anyspec, anyspec, anyspec),
        scratch_shapes=[
            pltpu.VMEM(st, jnp.float32),
            pltpu.VMEM(st, jnp.float32),
            pltpu.VMEM((len(near),) + st, jnp.float32),
            pltpu.VMEM((len(near),) + st, jnp.float32),
            pltpu.VMEM((nrecv,) + st, jnp.float32),
            pltpu.VMEM((nrecv,) + st, jnp.float32),
            pltpu.VMEM(st, jnp.float32),
            pltpu.VMEM(st, jnp.float32),
            pltpu.VMEM((4, seg_len, width), jnp.float32),
            pltpu.VMEM((4, seg_len, width), jnp.bfloat16),
            pltpu.VMEM((num_heads, seg_len, seg_len), jnp.bfloat16),
            pltpu.VMEM((num_heads, seg_len, seg_len), jnp.bfloat16),
            pltpu.SemaphoreType.DMA((2, num_heads, 2 * nrecv)),
            pltpu.SemaphoreType.DMA((4, num_heads, ne)),
            pltpu.SemaphoreType.DMA((4, num_heads, ne)),
            pltpu.SemaphoreType.DMA((4, num_heads)),
        ],
        compiler_params=pltpu.CompilerParams(
            collective_id=0, has_side_effects=True, vmem_limit_bytes=56 * 1024 * 1024
        ),
    )(decay_rate.astype(jnp.float32), query_tok, key_tok, value_tok, grad_out)


def solution(mesh):
    placed = (P("seq", "exp"), P("seq", "exp"), P("seq", "exp"), P("seq", "exp"), P("exp"))
    return jax.shard_map(
        shards,
        mesh=mesh,
        in_specs=placed,
        out_specs=(
            P(("seq", "exp"), None),
            P(("seq", "exp"), None),
            P(("seq", "exp"), None),
            P(("seq", "exp"), None),
        ),
        check_vma=False,
    )
```

```python
import functools

import jax
import jax.numpy as jnp
from jax import lax
from jax.experimental import pallas as pl
from jax.experimental.pallas import tpu as pltpu
from jax.sharding import PartitionSpec as P


MESH = pl.DeviceIdType.MESH


def whole_kernel(n, near, far, top, total, dec_ref, q_ref, k_ref, v_ref, do_ref,
                 o0, o1, o2, o3, dk_ref, dq_ref, kx, qx, krecv, qrecv, s_acc, r_acc, intra, stage, wts, gwts,
                 scan_sems, send_sems, recv_sems, local_sems):
    outs = (o0, o1, o2, o3)
    me_s = lax.axis_index("seq")
    me = lax.axis_index("exp")
    ne = lax.axis_size("exp")
    length, width = q_ref.shape
    heads = dec_ref.shape[0]
    hd = width // heads
    slab = length // ne
    blk = min(256, length)
    nblk = length // blk
    hi = lax.Precision.HIGHEST
    f32 = jnp.float32
    nt = (((1,), (1,)), ((), ()))
    tn = (((0,), (0,)), ((), ()))

    def cols(h):
        return pl.ds(h * hd, hd)

    rates = [jnp.full((1, 1), dec_ref[h], f32) for h in range(heads)]
    scales = [jnp.sqrt((2.0 * rates[h] + 2.0 / total) / hd) for h in range(heads)]
    wv = [[jnp.exp(-float(d) * (rates[h] * float(length))) for h in range(heads)] for d in near + [top]]
    place = lax.broadcasted_iota(jnp.int32, (length, 1), 0).astype(f32)
    for h in range(heads):
        rate = rates[h]
        keyed = (k_ref[:, cols(h)].astype(f32) * jnp.exp(-rate * (length - place))).astype(jnp.bfloat16)
        dk_ref[h] = lax.dot_general(keyed, v_ref[:, cols(h)], tn, preferred_element_type=f32)
        queried = (q_ref[:, cols(h)].astype(f32) * jnp.exp(-rate * (place + 1.0))).astype(jnp.bfloat16)
        dq_ref[h] = lax.dot_general(queried, do_ref[:, cols(h)], tn, preferred_element_type=f32)

    barrier = pltpu.get_barrier_semaphore()
    partners = sorted(set(near + [1, far]))
    peers = ne - 1
    for d in partners:
        for other in (me_s + d, me_s - d):
            @pl.when(jnp.logical_and(other >= 0, other < n))
            def _():
                pl.semaphore_signal(barrier, 1, device_id=(other, me), device_id_type=MESH)
            peers = peers + jnp.logical_and(other >= 0, other < n).astype(jnp.int32)
    for j in range(1, ne):
        pl.semaphore_signal(barrier, 1, device_id=(me_s, lax.rem(me + j, ne)), device_id_type=MESH)
    pl.semaphore_wait(barrier, peers)

    def weights_task(h):
        def run():
            rate = rates[h]
            scale = scales[h]
            qh = q_ref[:, cols(h)]
            kh = k_ref[:, cols(h)]
            vh = v_ref[:, cols(h)]
            dh = do_ref[:, cols(h)]
            for b in range(nblk):
                rows = pl.ds(b * blk, blk)
                i = (lax.broadcasted_iota(jnp.int32, (blk, length), 0) + b * blk).astype(f32)
                jj = lax.broadcasted_iota(jnp.int32, (blk, length), 1).astype(f32)
                off = i - jj
                damp = jnp.where(off >= 0, jnp.exp(-rate * jnp.maximum(off, 0.0)), 0.0) * scale
                sc = lax.dot_general(qh[b * blk:(b + 1) * blk], kh, nt, preferred_element_type=f32)
                wts[h, rows, :] = (sc * damp).astype(jnp.bfloat16)
                gs = lax.dot_general(dh[b * blk:(b + 1) * blk], vh, nt, preferred_element_type=f32)
                gwts[h, rows, :] = (gs * damp).astype(jnp.bfloat16)
        return run

    def intra_task(h, o):
        def run():
            for b in range(nblk):
                rows = pl.ds(b * blk, blk)
                if o == 0:
                    res = jnp.dot(wts[h, rows, :], v_ref[:, cols(h)], preferred_element_type=f32)
                elif o == 1:
                    res = jnp.dot(gwts[h, rows, :], k_ref[:, cols(h)], preferred_element_type=f32)
                elif o == 2:
                    res = lax.dot_general(gwts[h, :, rows], q_ref[:, cols(h)], tn, preferred_element_type=f32)
                else:
                    res = lax.dot_general(wts[h, :, rows], do_ref[:, cols(h)], tn, preferred_element_type=f32)
                intra[o, rows, cols(h)] = res
        return run

    def copy(src, dst, h, slot, other):
        return pltpu.make_async_remote_copy(
            src_ref=src, dst_ref=dst, send_sem=scan_sems.at[0, h, slot], recv_sem=scan_sems.at[1, h, slot],
            device_id=(lax.rem(other + n, n), me), device_id_type=MESH,
        )

    order = []
    for j in range(1, ne):
        for cand in (j, ne - j):
            if 0 < cand < ne and cand not in order:
                order.append(cand)

    def send(o, h):
        for j in order:
            peer = lax.rem(me + j, ne)
            pltpu.make_async_remote_copy(
                src_ref=stage.at[o, pl.ds(pl.multiple_of(peer * slab, slab), slab), cols(h)],
                dst_ref=outs[o].at[:, pl.ds(pl.multiple_of(me * width + h * hd, hd), hd)],
                send_sem=send_sems.at[o, h, j], recv_sem=recv_sems.at[o, h, j],
                device_id=(me_s, peer), device_id_type=MESH,
            ).start()
        pltpu.make_async_copy(
            stage.at[o, pl.ds(pl.multiple_of(me * slab, slab), slab), cols(h)],
            outs[o].at[:, pl.ds(pl.multiple_of(me * width + h * hd, hd), hd)],
            local_sems.at[o, h],
        ).start()

    def pos(b):
        return (lax.broadcasted_iota(jnp.int32, (blk, 1), 0) + b * blk).astype(f32)

    nround = len(near) + 1
    sent = []
    last = len(near)
    pending = []

    def flush_one():
        if pending:
            pending.pop(0)()

    for h in range(heads):
        mine = [weights_task(h)] + [intra_task(h, o) for o in range(4)]
        per_round = -(-len(mine) // nround)
        kcur, qcur = dk_ref.at[h], dq_ref.at[h]
        for r, d in enumerate(near):
            kc = copy(kcur, krecv.at[r, h], h, 2 * r, me_s + d)
            qc = copy(qcur, qrecv.at[r, h], h, 2 * r + 1, me_s - d)
            pl.when(me_s + d < n)(kc.start)
            pl.when(me_s - d >= 0)(qc.start)
            sent.append((kc, me_s + d < n))
            sent.append((qc, me_s - d >= 0))
            flush_one()
            for task in mine[r * per_round:(r + 1) * per_round]:
                task()
            for cur, nxt, recv, cp, has in ((kcur, kx, krecv, kc, me_s - d >= 0), (qcur, qx, qrecv, qc, me_s + d < n)):
                @pl.when(has)
                def _():
                    cp.wait_recv()
                    nxt[r, h] = cur[...] + wv[r][h] * recv[r, h]

                @pl.when(jnp.logical_not(has))
                def _():
                    nxt[r, h] = cur[...]
            kcur, qcur = kx.at[r, h], qx.at[r, h]
        finals = []
        for j, d in enumerate((1, far)):
            slot = 2 * (last + j)
            kc = copy(kcur, krecv.at[last + j, h], h, slot, me_s + d)
            qc = copy(qcur, qrecv.at[last + j, h], h, slot + 1, me_s - d)
            pl.when(me_s + d < n)(kc.start)
            pl.when(me_s - d >= 0)(qc.start)
            sent.append((kc, me_s + d < n))
            sent.append((qc, me_s - d >= 0))
            finals.append((kc, qc, d))
        flush_one()
        for task in mine[last * per_round:]:
            task()
        s_acc[h] = jnp.zeros((hd, hd), f32)
        r_acc[h] = jnp.zeros((hd, hd), f32)
        for j, (kc, qc, d) in enumerate(finals):
            for cp, recv, acc, has in ((kc, krecv, s_acc, me_s - d >= 0), (qc, qrecv, r_acc, me_s + d < n)):
                @pl.when(has)
                def _():
                    cp.wait_recv()
                    scale = 1.0 if j == 0 else wv[last][h]
                    acc[h] = acc[h] + scale * recv[last + j, h]

        def stage_send(h, o):
            def run():
                rate = rates[h]
                scale = scales[h]
                for b in range(nblk):
                    rows = pl.ds(b * blk, blk)
                    if o == 0:
                        lead = scale * jnp.exp(-rate * pos(b))
                        extra = lead * jnp.dot(q_ref[rows, cols(h)].astype(f32), s_acc[h], precision=hi, preferred_element_type=f32)
                    elif o == 1:
                        lead = scale * jnp.exp(-rate * pos(b))
                        extra = lead * lax.dot_general(do_ref[rows, cols(h)].astype(f32), s_acc[h], nt, precision=hi, preferred_element_type=f32)
                    elif o == 2:
                        trail = scale * jnp.exp(-rate * (length - 1.0 - pos(b)))
                        extra = trail * lax.dot_general(v_ref[rows, cols(h)].astype(f32), r_acc[h], nt, precision=hi, preferred_element_type=f32)
                    else:
                        trail = scale * jnp.exp(-rate * (length - 1.0 - pos(b)))
                        extra = trail * jnp.dot(k_ref[rows, cols(h)].astype(f32), r_acc[h], precision=hi, preferred_element_type=f32)
                    stage[o, rows, cols(h)] = (intra[o, rows, cols(h)] + extra).astype(jnp.bfloat16)
                send(o, h)
            return run

        batches = [stage_send(h, o) for o in range(4)]
        if h < heads - 1:
            batches[0]()
            pending.extend(batches[1:])
        else:
            while pending:
                flush_one()
            for run in batches:
                run()

    for cp, cond in sent:
        pl.when(cond)(cp.wait_send)
    for o in range(4):
        for h in range(heads):
            for j in range(1, ne):
                cp = pltpu.make_async_remote_copy(
                    src_ref=stage.at[o, pl.ds(0, slab), cols(h)],
                    dst_ref=outs[o].at[:, pl.ds(h * hd, hd)],
                    send_sem=send_sems.at[o, h, j], recv_sem=recv_sems.at[o, h, j],
                    device_id=(me_s, lax.rem(me + j, ne)), device_id_type=MESH,
                )
                cp.wait_send()
                cp.wait_recv()
            pltpu.make_async_copy(
                stage.at[o, pl.ds(0, slab), cols(h)], outs[o].at[:, pl.ds(h * hd, hd)], local_sems.at[o, h]
            ).wait()


def settle_kernel(a, b, c, d, oa, ob, oc, od):
    for src, dst in ((a, oa), (b, ob), (c, oc), (d, od)):
        dst[...] = src[...]


def shards(query_tok, key_tok, value_tok, grad_out, decay_rate):
    seg_len = query_tok.shape[0]
    num_heads = decay_rate.shape[0]
    head_size = query_tok.shape[1] // num_heads
    ne = lax.axis_size("exp")
    total_len = seg_len * lax.axis_size("seq")
    n = lax.axis_size("seq")
    near = []
    d = 1
    while 2 * d < n:
        near.append(d)
        d *= 2
    far = d + 1
    nrecv = len(near) + 2
    width = query_tok.shape[1]
    slab = seg_len // ne
    out = jax.ShapeDtypeStruct((slab, ne * width), jnp.bfloat16)
    smem = pl.BlockSpec(memory_space=pltpu.SMEM)
    vspec = pl.BlockSpec(memory_space=pltpu.VMEM)
    anyspec = pl.BlockSpec(memory_space=pl.ANY)
    st = (num_heads, head_size, head_size)
    moved = pl.pallas_call(
        functools.partial(whole_kernel, n, near, far, d, total_len),
        out_shape=(out, out, out, out),
        in_specs=[smem] + [vspec] * 4,
        out_specs=(anyspec, anyspec, anyspec, anyspec),
        scratch_shapes=[
            pltpu.VMEM(st, jnp.float32),
            pltpu.VMEM(st, jnp.float32),
            pltpu.VMEM((len(near),) + st, jnp.float32),
            pltpu.VMEM((len(near),) + st, jnp.float32),
            pltpu.VMEM((nrecv,) + st, jnp.float32),
            pltpu.VMEM((nrecv,) + st, jnp.float32),
            pltpu.VMEM(st, jnp.float32),
            pltpu.VMEM(st, jnp.float32),
            pltpu.VMEM((4, seg_len, width), jnp.float32),
            pltpu.VMEM((4, seg_len, width), jnp.bfloat16),
            pltpu.VMEM((num_heads, seg_len, seg_len), jnp.bfloat16),
            pltpu.VMEM((num_heads, seg_len, seg_len), jnp.bfloat16),
            pltpu.SemaphoreType.DMA((2, num_heads, 2 * nrecv)),
            pltpu.SemaphoreType.DMA((4, num_heads, ne)),
            pltpu.SemaphoreType.DMA((4, num_heads, ne)),
            pltpu.SemaphoreType.DMA((4, num_heads)),
        ],
        compiler_params=pltpu.CompilerParams(
            collective_id=0, has_side_effects=True, vmem_limit_bytes=56 * 1024 * 1024
        ),
    )(decay_rate.astype(jnp.float32), query_tok, key_tok, value_tok, grad_out)
    return pl.pallas_call(
        settle_kernel,
        out_shape=(out, out, out, out),
        in_specs=[vspec] * 4,
        out_specs=(vspec, vspec, vspec, vspec),
    )(*moved)


def solution(mesh):
    placed = (P("seq", "exp"), P("seq", "exp"), P("seq", "exp"), P("seq", "exp"), P("exp"))
    return jax.shard_map(
        shards,
        mesh=mesh,
        in_specs=placed,
        out_specs=(
            P(("seq", "exp"), None),
            P(("seq", "exp"), None),
            P(("seq", "exp"), None),
            P(("seq", "exp"), None),
        ),
        check_vma=False,
    )
```

```python
import functools

import jax
import jax.numpy as jnp
from jax import lax
from jax.experimental import pallas as pl
from jax.experimental.pallas import tpu as pltpu
from jax.sharding import PartitionSpec as P


MESH = pl.DeviceIdType.MESH


def whole_kernel(n, near, far, top, total, dec_ref, q_ref, k_ref, v_ref, do_ref,
                 o0, o1, o2, o3, dk_ref, dq_ref, kx, qx, krecv, qrecv, s_acc, r_acc, intra, stage, wts, gwts,
                 scan_sems, send_sems, recv_sems, local_sems):
    outs = (o0, o1, o2, o3)
    me_s = lax.axis_index("seq")
    me = lax.axis_index("exp")
    ne = lax.axis_size("exp")
    length, width = q_ref.shape
    heads = dec_ref.shape[0]
    hd = width // heads
    slab = length // ne
    blk = min(256, length)
    nblk = length // blk
    hi = lax.Precision.HIGHEST
    f32 = jnp.float32
    nt = (((1,), (1,)), ((), ()))
    tn = (((0,), (0,)), ((), ()))

    def cols(h):
        return pl.ds(h * hd, hd)

    rates = [jnp.full((1, 1), dec_ref[h], f32) for h in range(heads)]
    scales = [jnp.sqrt((2.0 * rates[h] + 2.0 / total) / hd) for h in range(heads)]
    wv = [[jnp.exp(-float(d) * (rates[h] * float(length))) for h in range(heads)] for d in near + [top]]
    place = lax.broadcasted_iota(jnp.int32, (length, 1), 0).astype(f32)
    for h in range(heads):
        rate = rates[h]
        keyed = (k_ref[:, cols(h)].astype(f32) * jnp.exp(-rate * (length - place))).astype(jnp.bfloat16)
        dk_ref[h] = lax.dot_general(keyed, v_ref[:, cols(h)], tn, preferred_element_type=f32)
        queried = (q_ref[:, cols(h)].astype(f32) * jnp.exp(-rate * (place + 1.0))).astype(jnp.bfloat16)
        dq_ref[h] = lax.dot_general(queried, do_ref[:, cols(h)], tn, preferred_element_type=f32)

    barrier = pltpu.get_barrier_semaphore()
    partners = sorted(set(near + [1, far]))
    peers = ne - 1
    for d in partners:
        for other in (me_s + d, me_s - d):
            @pl.when(jnp.logical_and(other >= 0, other < n))
            def _():
                pl.semaphore_signal(barrier, 1, device_id=(other, me), device_id_type=MESH)
            peers = peers + jnp.logical_and(other >= 0, other < n).astype(jnp.int32)
    for j in range(1, ne):
        pl.semaphore_signal(barrier, 1, device_id=(me_s, lax.rem(me + j, ne)), device_id_type=MESH)
    pl.semaphore_wait(barrier, peers)

    def weights_task(h):
        def run():
            rate = rates[h]
            scale = scales[h]
            qh = q_ref[:, cols(h)]
            kh = k_ref[:, cols(h)]
            vh = v_ref[:, cols(h)]
            dh = do_ref[:, cols(h)]
            for b in range(nblk):
                rows = pl.ds(b * blk, blk)
                i = (lax.broadcasted_iota(jnp.int32, (blk, length), 0) + b * blk).astype(f32)
                jj = lax.broadcasted_iota(jnp.int32, (blk, length), 1).astype(f32)
                off = i - jj
                damp = jnp.where(off >= 0, jnp.exp(-rate * jnp.maximum(off, 0.0)), 0.0) * scale
                sc = lax.dot_general(qh[b * blk:(b + 1) * blk], kh, nt, preferred_element_type=f32)
                wts[h, rows, :] = (sc * damp).astype(jnp.bfloat16)
                gs = lax.dot_general(dh[b * blk:(b + 1) * blk], vh, nt, preferred_element_type=f32)
                gwts[h, rows, :] = (gs * damp).astype(jnp.bfloat16)
        return run

    def intra_task(h, o):
        def run():
            for b in range(nblk):
                rows = pl.ds(b * blk, blk)
                if o == 0:
                    res = jnp.dot(wts[h, rows, :], v_ref[:, cols(h)], preferred_element_type=f32)
                elif o == 1:
                    res = jnp.dot(gwts[h, rows, :], k_ref[:, cols(h)], preferred_element_type=f32)
                elif o == 2:
                    res = lax.dot_general(gwts[h, :, rows], q_ref[:, cols(h)], tn, preferred_element_type=f32)
                else:
                    res = lax.dot_general(wts[h, :, rows], do_ref[:, cols(h)], tn, preferred_element_type=f32)
                intra[o, rows, cols(h)] = res
        return run

    def copy(src, dst, h, slot, other):
        return pltpu.make_async_remote_copy(
            src_ref=src, dst_ref=dst, send_sem=scan_sems.at[0, h, slot], recv_sem=scan_sems.at[1, h, slot],
            device_id=(lax.rem(other + n, n), me), device_id_type=MESH,
        )

    order = []
    for j in range(1, ne):
        for cand in (j, ne - j):
            if 0 < cand < ne and cand not in order:
                order.append(cand)

    def send(o, h):
        for j in order:
            peer = lax.rem(me + j, ne)
            pltpu.make_async_remote_copy(
                src_ref=stage.at[o, pl.ds(pl.multiple_of(peer * slab, slab), slab), cols(h)],
                dst_ref=outs[o].at[:, pl.ds(pl.multiple_of(me * width + h * hd, hd), hd)],
                send_sem=send_sems.at[o, h, j], recv_sem=recv_sems.at[o, h, j],
                device_id=(me_s, peer), device_id_type=MESH,
            ).start()
        pltpu.make_async_copy(
            stage.at[o, pl.ds(pl.multiple_of(me * slab, slab), slab), cols(h)],
            outs[o].at[:, pl.ds(pl.multiple_of(me * width + h * hd, hd), hd)],
            local_sems.at[o, h],
        ).start()

    def pos(b):
        return (lax.broadcasted_iota(jnp.int32, (blk, 1), 0) + b * blk).astype(f32)

    nround = len(near) + 1
    sent = []
    last = len(near)
    pending = []

    def flush_one():
        if pending:
            pending.pop(0)()

    for h in range(heads):
        mine = [weights_task(h)] + [intra_task(h, o) for o in range(4)]
        per_round = -(-len(mine) // nround)
        kcur, qcur = dk_ref.at[h], dq_ref.at[h]
        for r, d in enumerate(near):
            kc = copy(kcur, krecv.at[r, h], h, 2 * r, me_s + d)
            qc = copy(qcur, qrecv.at[r, h], h, 2 * r + 1, me_s - d)
            pl.when(me_s + d < n)(kc.start)
            pl.when(me_s - d >= 0)(qc.start)
            sent.append((kc, me_s + d < n))
            sent.append((qc, me_s - d >= 0))
            flush_one()
            for task in mine[r * per_round:(r + 1) * per_round]:
                task()
            for cur, nxt, recv, cp, has in ((kcur, kx, krecv, kc, me_s - d >= 0), (qcur, qx, qrecv, qc, me_s + d < n)):
                @pl.when(has)
                def _():
                    cp.wait_recv()
                    nxt[r, h] = cur[...] + wv[r][h] * recv[r, h]

                @pl.when(jnp.logical_not(has))
                def _():
                    nxt[r, h] = cur[...]
            kcur, qcur = kx.at[r, h], qx.at[r, h]
        finals = []
        for j, d in enumerate((1, far)):
            slot = 2 * (last + j)
            kc = copy(kcur, krecv.at[last + j, h], h, slot, me_s + d)
            qc = copy(qcur, qrecv.at[last + j, h], h, slot + 1, me_s - d)
            pl.when(me_s + d < n)(kc.start)
            pl.when(me_s - d >= 0)(qc.start)
            sent.append((kc, me_s + d < n))
            sent.append((qc, me_s - d >= 0))
            finals.append((kc, qc, d))
        flush_one()
        for task in mine[last * per_round:]:
            task()
        s_acc[h] = jnp.zeros((hd, hd), f32)
        r_acc[h] = jnp.zeros((hd, hd), f32)
        for j, (kc, qc, d) in enumerate(finals):
            for cp, recv, acc, has in ((kc, krecv, s_acc, me_s - d >= 0), (qc, qrecv, r_acc, me_s + d < n)):
                @pl.when(has)
                def _():
                    cp.wait_recv()
                    scale = 1.0 if j == 0 else wv[last][h]
                    acc[h] = acc[h] + scale * recv[last + j, h]

        def stage_send(h, o):
            def run():
                rate = rates[h]
                scale = scales[h]
                for b in range(nblk):
                    rows = pl.ds(b * blk, blk)
                    if o == 0:
                        lead = scale * jnp.exp(-rate * pos(b))
                        extra = lead * jnp.dot(q_ref[rows, cols(h)].astype(f32), s_acc[h], precision=hi, preferred_element_type=f32)
                    elif o == 1:
                        lead = scale * jnp.exp(-rate * pos(b))
                        extra = lead * lax.dot_general(do_ref[rows, cols(h)].astype(f32), s_acc[h], nt, precision=hi, preferred_element_type=f32)
                    elif o == 2:
                        trail = scale * jnp.exp(-rate * (length - 1.0 - pos(b)))
                        extra = trail * lax.dot_general(v_ref[rows, cols(h)].astype(f32), r_acc[h], nt, precision=hi, preferred_element_type=f32)
                    else:
                        trail = scale * jnp.exp(-rate * (length - 1.0 - pos(b)))
                        extra = trail * jnp.dot(k_ref[rows, cols(h)].astype(f32), r_acc[h], precision=hi, preferred_element_type=f32)
                    stage[o, rows, cols(h)] = (intra[o, rows, cols(h)] + extra).astype(jnp.bfloat16)
                send(o, h)
            return run

        batches = [stage_send(h, o) for o in range(4)]
        if h < heads - 1:
            batches[0]()
            pending.extend(batches[1:])
        else:
            while pending:
                flush_one()
            for run in batches:
                run()

    for cp, cond in sent:
        pl.when(cond)(cp.wait_send)
    for o in range(4):
        for h in range(heads):
            for j in range(1, ne):
                cp = pltpu.make_async_remote_copy(
                    src_ref=stage.at[o, pl.ds(0, slab), cols(h)],
                    dst_ref=outs[o].at[:, pl.ds(h * hd, hd)],
                    send_sem=send_sems.at[o, h, j], recv_sem=recv_sems.at[o, h, j],
                    device_id=(me_s, lax.rem(me + j, ne)), device_id_type=MESH,
                )
                cp.wait_send()
                cp.wait_recv()
            pltpu.make_async_copy(
                stage.at[o, pl.ds(0, slab), cols(h)], outs[o].at[:, pl.ds(h * hd, hd)], local_sems.at[o, h]
            ).wait()


def settle_kernel(a, b, c, d, oa, ob, oc, od, buf, sems):
    pairs = ((a, oa), (b, ob), (c, oc), (d, od))
    loads = [pltpu.make_async_copy(src, buf.at[i], sems.at[0, i]) for i, (src, _) in enumerate(pairs)]
    for cp in loads:
        cp.start()
    stores = []
    for i, (_, dst) in enumerate(pairs):
        loads[i].wait()
        cp = pltpu.make_async_copy(buf.at[i], dst, sems.at[1, i])
        cp.start()
        stores.append(cp)
    for cp in stores:
        cp.wait()


def shards(query_tok, key_tok, value_tok, grad_out, decay_rate):
    seg_len = query_tok.shape[0]
    num_heads = decay_rate.shape[0]
    head_size = query_tok.shape[1] // num_heads
    ne = lax.axis_size("exp")
    total_len = seg_len * lax.axis_size("seq")
    n = lax.axis_size("seq")
    near = []
    d = 1
    while 2 * d < n:
        near.append(d)
        d *= 2
    far = d + 1
    nrecv = len(near) + 2
    width = query_tok.shape[1]
    slab = seg_len // ne
    out = jax.ShapeDtypeStruct((slab, ne * width), jnp.bfloat16)
    smem = pl.BlockSpec(memory_space=pltpu.SMEM)
    vspec = pl.BlockSpec(memory_space=pltpu.VMEM)
    anyspec = pl.BlockSpec(memory_space=pl.ANY)
    st = (num_heads, head_size, head_size)
    moved = pl.pallas_call(
        functools.partial(whole_kernel, n, near, far, d, total_len),
        out_shape=(out, out, out, out),
        in_specs=[smem] + [vspec] * 4,
        out_specs=(anyspec, anyspec, anyspec, anyspec),
        scratch_shapes=[
            pltpu.VMEM(st, jnp.float32),
            pltpu.VMEM(st, jnp.float32),
            pltpu.VMEM((len(near),) + st, jnp.float32),
            pltpu.VMEM((len(near),) + st, jnp.float32),
            pltpu.VMEM((nrecv,) + st, jnp.float32),
            pltpu.VMEM((nrecv,) + st, jnp.float32),
            pltpu.VMEM(st, jnp.float32),
            pltpu.VMEM(st, jnp.float32),
            pltpu.VMEM((4, seg_len, width), jnp.float32),
            pltpu.VMEM((4, seg_len, width), jnp.bfloat16),
            pltpu.VMEM((num_heads, seg_len, seg_len), jnp.bfloat16),
            pltpu.VMEM((num_heads, seg_len, seg_len), jnp.bfloat16),
            pltpu.SemaphoreType.DMA((2, num_heads, 2 * nrecv)),
            pltpu.SemaphoreType.DMA((4, num_heads, ne)),
            pltpu.SemaphoreType.DMA((4, num_heads, ne)),
            pltpu.SemaphoreType.DMA((4, num_heads)),
        ],
        compiler_params=pltpu.CompilerParams(
            collective_id=0, has_side_effects=True, vmem_limit_bytes=56 * 1024 * 1024
        ),
    )(decay_rate.astype(jnp.float32), query_tok, key_tok, value_tok, grad_out)
    return pl.pallas_call(
        settle_kernel,
        out_shape=(out, out, out, out),
        in_specs=[anyspec] * 4,
        out_specs=(anyspec, anyspec, anyspec, anyspec),
        scratch_shapes=[pltpu.VMEM((4,) + out.shape, out.dtype), pltpu.SemaphoreType.DMA((2, 4))],
    )(*moved)


def solution(mesh):
    placed = (P("seq", "exp"), P("seq", "exp"), P("seq", "exp"), P("seq", "exp"), P("exp"))
    return jax.shard_map(
        shards,
        mesh=mesh,
        in_specs=placed,
        out_specs=(
            P(("seq", "exp"), None),
            P(("seq", "exp"), None),
            P(("seq", "exp"), None),
            P(("seq", "exp"), None),
        ),
        check_vma=False,
    )
```

```python
import functools

import jax
import jax.numpy as jnp
from jax import lax
from jax.experimental import pallas as pl
from jax.experimental.pallas import tpu as pltpu
from jax.sharding import PartitionSpec as P


MESH = pl.DeviceIdType.MESH


def whole_kernel(n, near, far, top, total, dec_ref, q_ref, k_ref, v_ref, do_ref,
                 o0, o1, o2, o3, dk_ref, dq_ref, kx, qx, krecv, qrecv, s_acc, r_acc, intra, stage, wts, gwts,
                 scan_sems, send_sems, recv_sems, local_sems):
    outs = (o0, o1, o2, o3)
    me_s = lax.axis_index("seq")
    me = lax.axis_index("exp")
    ne = lax.axis_size("exp")
    length, width = q_ref.shape
    heads = dec_ref.shape[0]
    hd = width // heads
    slab = length // ne
    blk = min(256, length)
    nblk = length // blk
    hi = lax.Precision.HIGHEST
    f32 = jnp.float32
    nt = (((1,), (1,)), ((), ()))
    tn = (((0,), (0,)), ((), ()))

    def cols(h):
        return pl.ds(h * hd, hd)

    rates = [jnp.full((1, 1), dec_ref[h], f32) for h in range(heads)]
    scales = [jnp.sqrt((2.0 * rates[h] + 2.0 / total) / hd) for h in range(heads)]
    wv = [[jnp.exp(-float(d) * (rates[h] * float(length))) for h in range(heads)] for d in near + [top]]
    place = lax.broadcasted_iota(jnp.int32, (length, 1), 0).astype(f32)
    def state_task(h):
        def run():
            rate = rates[h]
            keyed = (k_ref[:, cols(h)].astype(f32) * jnp.exp(-rate * (length - place))).astype(jnp.bfloat16)
            dk_ref[h] = lax.dot_general(keyed, v_ref[:, cols(h)], tn, preferred_element_type=f32)
            queried = (q_ref[:, cols(h)].astype(f32) * jnp.exp(-rate * (place + 1.0))).astype(jnp.bfloat16)
            dq_ref[h] = lax.dot_general(queried, do_ref[:, cols(h)], tn, preferred_element_type=f32)
        return run

    state_task(0)()

    barrier = pltpu.get_barrier_semaphore()
    partners = sorted(set(near + [1, far]))
    peers = ne - 1
    for d in partners:
        for other in (me_s + d, me_s - d):
            @pl.when(jnp.logical_and(other >= 0, other < n))
            def _():
                pl.semaphore_signal(barrier, 1, device_id=(other, me), device_id_type=MESH)
            peers = peers + jnp.logical_and(other >= 0, other < n).astype(jnp.int32)
    for j in range(1, ne):
        pl.semaphore_signal(barrier, 1, device_id=(me_s, lax.rem(me + j, ne)), device_id_type=MESH)
    pl.semaphore_wait(barrier, peers)

    def weights_task(h):
        def run():
            rate = rates[h]
            scale = scales[h]
            qh = q_ref[:, cols(h)]
            kh = k_ref[:, cols(h)]
            vh = v_ref[:, cols(h)]
            dh = do_ref[:, cols(h)]
            for b in range(nblk):
                rows = pl.ds(b * blk, blk)
                i = (lax.broadcasted_iota(jnp.int32, (blk, length), 0) + b * blk).astype(f32)
                jj = lax.broadcasted_iota(jnp.int32, (blk, length), 1).astype(f32)
                off = i - jj
                damp = jnp.where(off >= 0, jnp.exp(-rate * jnp.maximum(off, 0.0)), 0.0) * scale
                sc = lax.dot_general(qh[b * blk:(b + 1) * blk], kh, nt, preferred_element_type=f32)
                wts[h, rows, :] = (sc * damp).astype(jnp.bfloat16)
                gs = lax.dot_general(dh[b * blk:(b + 1) * blk], vh, nt, preferred_element_type=f32)
                gwts[h, rows, :] = (gs * damp).astype(jnp.bfloat16)
        return run

    def intra_task(h, o):
        def run():
            for b in range(nblk):
                rows = pl.ds(b * blk, blk)
                if o == 0:
                    res = jnp.dot(wts[h, rows, :], v_ref[:, cols(h)], preferred_element_type=f32)
                elif o == 1:
                    res = jnp.dot(gwts[h, rows, :], k_ref[:, cols(h)], preferred_element_type=f32)
                elif o == 2:
                    res = lax.dot_general(gwts[h, :, rows], q_ref[:, cols(h)], tn, preferred_element_type=f32)
                else:
                    res = lax.dot_general(wts[h, :, rows], do_ref[:, cols(h)], tn, preferred_element_type=f32)
                intra[o, rows, cols(h)] = res
        return run

    def copy(src, dst, h, slot, other):
        return pltpu.make_async_remote_copy(
            src_ref=src, dst_ref=dst, send_sem=scan_sems.at[0, h, slot], recv_sem=scan_sems.at[1, h, slot],
            device_id=(lax.rem(other + n, n), me), device_id_type=MESH,
        )

    order = []
    for j in range(1, ne):
        for cand in (j, ne - j):
            if 0 < cand < ne and cand not in order:
                order.append(cand)

    def send(o, h):
        for j in order:
            peer = lax.rem(me + j, ne)
            pltpu.make_async_remote_copy(
                src_ref=stage.at[o, pl.ds(pl.multiple_of(peer * slab, slab), slab), cols(h)],
                dst_ref=outs[o].at[:, pl.ds(pl.multiple_of(me * width + h * hd, hd), hd)],
                send_sem=send_sems.at[o, h, j], recv_sem=recv_sems.at[o, h, j],
                device_id=(me_s, peer), device_id_type=MESH,
            ).start()
        pltpu.make_async_copy(
            stage.at[o, pl.ds(pl.multiple_of(me * slab, slab), slab), cols(h)],
            outs[o].at[:, pl.ds(pl.multiple_of(me * width + h * hd, hd), hd)],
            local_sems.at[o, h],
        ).start()

    def pos(b):
        return (lax.broadcasted_iota(jnp.int32, (blk, 1), 0) + b * blk).astype(f32)

    nround = len(near) + 1
    sent = []
    last = len(near)
    pending = []

    def flush_one():
        if pending:
            pending.pop(0)()

    for h in range(heads):
        mine = [weights_task(h)] + [intra_task(h, o) for o in range(4)]
        if h == 0:
            mine = [state_task(g) for g in range(1, heads)] + mine
        per_round = -(-len(mine) // nround)
        kcur, qcur = dk_ref.at[h], dq_ref.at[h]
        for r, d in enumerate(near):
            kc = copy(kcur, krecv.at[r, h], h, 2 * r, me_s + d)
            qc = copy(qcur, qrecv.at[r, h], h, 2 * r + 1, me_s - d)
            pl.when(me_s + d < n)(kc.start)
            pl.when(me_s - d >= 0)(qc.start)
            sent.append((kc, me_s + d < n))
            sent.append((qc, me_s - d >= 0))
            flush_one()
            for task in mine[r * per_round:(r + 1) * per_round]:
                task()
            for cur, nxt, recv, cp, has in ((kcur, kx, krecv, kc, me_s - d >= 0), (qcur, qx, qrecv, qc, me_s + d < n)):
                @pl.when(has)
                def _():
                    cp.wait_recv()
                    nxt[r, h] = cur[...] + wv[r][h] * recv[r, h]

                @pl.when(jnp.logical_not(has))
                def _():
                    nxt[r, h] = cur[...]
            kcur, qcur = kx.at[r, h], qx.at[r, h]
        finals = []
        for j, d in enumerate((1, far)):
            slot = 2 * (last + j)
            kc = copy(kcur, krecv.at[last + j, h], h, slot, me_s + d)
            qc = copy(qcur, qrecv.at[last + j, h], h, slot + 1, me_s - d)
            pl.when(me_s + d < n)(kc.start)
            pl.when(me_s - d >= 0)(qc.start)
            sent.append((kc, me_s + d < n))
            sent.append((qc, me_s - d >= 0))
            finals.append((kc, qc, d))
        flush_one()
        for task in mine[last * per_round:]:
            task()
        s_acc[h] = jnp.zeros((hd, hd), f32)
        r_acc[h] = jnp.zeros((hd, hd), f32)
        for j, (kc, qc, d) in enumerate(finals):
            for cp, recv, acc, has in ((kc, krecv, s_acc, me_s - d >= 0), (qc, qrecv, r_acc, me_s + d < n)):
                @pl.when(has)
                def _():
                    cp.wait_recv()
                    scale = 1.0 if j == 0 else wv[last][h]
                    acc[h] = acc[h] + scale * recv[last + j, h]

        def stage_send(h, o):
            def run():
                rate = rates[h]
                scale = scales[h]
                for b in range(nblk):
                    rows = pl.ds(b * blk, blk)
                    if o == 0:
                        lead = scale * jnp.exp(-rate * pos(b))
                        extra = lead * jnp.dot(q_ref[rows, cols(h)].astype(f32), s_acc[h], precision=hi, preferred_element_type=f32)
                    elif o == 1:
                        lead = scale * jnp.exp(-rate * pos(b))
                        extra = lead * lax.dot_general(do_ref[rows, cols(h)].astype(f32), s_acc[h], nt, precision=hi, preferred_element_type=f32)
                    elif o == 2:
                        trail = scale * jnp.exp(-rate * (length - 1.0 - pos(b)))
                        extra = trail * lax.dot_general(v_ref[rows, cols(h)].astype(f32), r_acc[h], nt, precision=hi, preferred_element_type=f32)
                    else:
                        trail = scale * jnp.exp(-rate * (length - 1.0 - pos(b)))
                        extra = trail * jnp.dot(k_ref[rows, cols(h)].astype(f32), r_acc[h], precision=hi, preferred_element_type=f32)
                    stage[o, rows, cols(h)] = (intra[o, rows, cols(h)] + extra).astype(jnp.bfloat16)
                send(o, h)
            return run

        batches = [stage_send(h, o) for o in range(4)]
        if h < heads - 1:
            batches[0]()
            pending.extend(batches[1:])
        else:
            while pending:
                flush_one()
            for run in batches:
                run()

    for cp, cond in sent:
        pl.when(cond)(cp.wait_send)
    for o in range(4):
        for h in range(heads):
            for j in range(1, ne):
                cp = pltpu.make_async_remote_copy(
                    src_ref=stage.at[o, pl.ds(0, slab), cols(h)],
                    dst_ref=outs[o].at[:, pl.ds(h * hd, hd)],
                    send_sem=send_sems.at[o, h, j], recv_sem=recv_sems.at[o, h, j],
                    device_id=(me_s, lax.rem(me + j, ne)), device_id_type=MESH,
                )
                cp.wait_send()
                cp.wait_recv()
            pltpu.make_async_copy(
                stage.at[o, pl.ds(0, slab), cols(h)], outs[o].at[:, pl.ds(h * hd, hd)], local_sems.at[o, h]
            ).wait()


def settle_kernel(a, b, c, d, oa, ob, oc, od):
    for src, dst in ((a, oa), (b, ob), (c, oc), (d, od)):
        dst[...] = src[...]


def shards(query_tok, key_tok, value_tok, grad_out, decay_rate):
    seg_len = query_tok.shape[0]
    num_heads = decay_rate.shape[0]
    head_size = query_tok.shape[1] // num_heads
    ne = lax.axis_size("exp")
    total_len = seg_len * lax.axis_size("seq")
    n = lax.axis_size("seq")
    near = []
    d = 1
    while 2 * d < n:
        near.append(d)
        d *= 2
    far = d + 1
    nrecv = len(near) + 2
    width = query_tok.shape[1]
    slab = seg_len // ne
    out = jax.ShapeDtypeStruct((slab, ne * width), jnp.bfloat16)
    smem = pl.BlockSpec(memory_space=pltpu.SMEM)
    vspec = pl.BlockSpec(memory_space=pltpu.VMEM)
    anyspec = pl.BlockSpec(memory_space=pl.ANY)
    st = (num_heads, head_size, head_size)
    moved = pl.pallas_call(
        functools.partial(whole_kernel, n, near, far, d, total_len),
        out_shape=(out, out, out, out),
        in_specs=[smem] + [vspec] * 4,
        out_specs=(anyspec, anyspec, anyspec, anyspec),
        scratch_shapes=[
            pltpu.VMEM(st, jnp.float32),
            pltpu.VMEM(st, jnp.float32),
            pltpu.VMEM((len(near),) + st, jnp.float32),
            pltpu.VMEM((len(near),) + st, jnp.float32),
            pltpu.VMEM((nrecv,) + st, jnp.float32),
            pltpu.VMEM((nrecv,) + st, jnp.float32),
            pltpu.VMEM(st, jnp.float32),
            pltpu.VMEM(st, jnp.float32),
            pltpu.VMEM((4, seg_len, width), jnp.float32),
            pltpu.VMEM((4, seg_len, width), jnp.bfloat16),
            pltpu.VMEM((num_heads, seg_len, seg_len), jnp.bfloat16),
            pltpu.VMEM((num_heads, seg_len, seg_len), jnp.bfloat16),
            pltpu.SemaphoreType.DMA((2, num_heads, 2 * nrecv)),
            pltpu.SemaphoreType.DMA((4, num_heads, ne)),
            pltpu.SemaphoreType.DMA((4, num_heads, ne)),
            pltpu.SemaphoreType.DMA((4, num_heads)),
        ],
        compiler_params=pltpu.CompilerParams(
            collective_id=0, has_side_effects=True, vmem_limit_bytes=56 * 1024 * 1024
        ),
    )(decay_rate.astype(jnp.float32), query_tok, key_tok, value_tok, grad_out)
    return pl.pallas_call(
        settle_kernel,
        out_shape=(out, out, out, out),
        in_specs=[vspec] * 4,
        out_specs=(vspec, vspec, vspec, vspec),
    )(*moved)


def solution(mesh):
    placed = (P("seq", "exp"), P("seq", "exp"), P("seq", "exp"), P("seq", "exp"), P("exp"))
    return jax.shard_map(
        shards,
        mesh=mesh,
        in_specs=placed,
        out_specs=(
            P(("seq", "exp"), None),
            P(("seq", "exp"), None),
            P(("seq", "exp"), None),
            P(("seq", "exp"), None),
        ),
        check_vma=False,
    )
```

```python
import functools

import jax
import jax.numpy as jnp
from jax import lax
from jax.experimental import pallas as pl
from jax.experimental.pallas import tpu as pltpu
from jax.sharding import PartitionSpec as P


MESH = pl.DeviceIdType.MESH


def whole_kernel(n, near, far, top, total, dec_ref, q_ref, k_ref, v_ref, do_ref,
                 o0, o1, o2, o3, dk_ref, dq_ref, kx, qx, krecv, qrecv, s_acc, r_acc, intra, stage, wts, gwts,
                 scan_sems, send_sems, recv_sems, local_sems):
    outs = (o0, o1, o2, o3)
    me_s = lax.axis_index("seq")
    me = lax.axis_index("exp")
    ne = lax.axis_size("exp")
    length, width = q_ref.shape
    heads = dec_ref.shape[0]
    hd = width // heads
    slab = length // ne
    blk = min(256, length)
    nblk = length // blk
    hi = lax.Precision.HIGHEST
    f32 = jnp.float32
    nt = (((1,), (1,)), ((), ()))
    tn = (((0,), (0,)), ((), ()))

    def cols(h):
        return pl.ds(h * hd, hd)

    rates = [jnp.full((1, 1), dec_ref[h], f32) for h in range(heads)]
    scales = [jnp.sqrt((2.0 * rates[h] + 2.0 / total) / hd) for h in range(heads)]
    wv = [[jnp.exp(-float(d) * (rates[h] * float(length))) for h in range(heads)] for d in near + [top]]
    place = lax.broadcasted_iota(jnp.int32, (length, 1), 0).astype(f32)
    def state_task(h):
        def run():
            rate = rates[h]
            keyed = (k_ref[:, cols(h)].astype(f32) * jnp.exp(-rate * (length - place))).astype(jnp.bfloat16)
            dk_ref[h] = lax.dot_general(keyed, v_ref[:, cols(h)], tn, preferred_element_type=f32)
            queried = (q_ref[:, cols(h)].astype(f32) * jnp.exp(-rate * (place + 1.0))).astype(jnp.bfloat16)
            dq_ref[h] = lax.dot_general(queried, do_ref[:, cols(h)], tn, preferred_element_type=f32)
        return run


    barrier = pltpu.get_barrier_semaphore()
    partners = sorted(set(near + [1, far]))
    peers = ne - 1
    for d in partners:
        for other in (me_s + d, me_s - d):
            @pl.when(jnp.logical_and(other >= 0, other < n))
            def _():
                pl.semaphore_signal(barrier, 1, device_id=(other, me), device_id_type=MESH)
            peers = peers + jnp.logical_and(other >= 0, other < n).astype(jnp.int32)
    for j in range(1, ne):
        pl.semaphore_signal(barrier, 1, device_id=(me_s, lax.rem(me + j, ne)), device_id_type=MESH)
    state_task(0)()
    pl.semaphore_wait(barrier, peers)

    def weights_task(h):
        def run():
            rate = rates[h]
            scale = scales[h]
            qh = q_ref[:, cols(h)]
            kh = k_ref[:, cols(h)]
            vh = v_ref[:, cols(h)]
            dh = do_ref[:, cols(h)]
            for b in range(nblk):
                rows = pl.ds(b * blk, blk)
                i = (lax.broadcasted_iota(jnp.int32, (blk, length), 0) + b * blk).astype(f32)
                jj = lax.broadcasted_iota(jnp.int32, (blk, length), 1).astype(f32)
                off = i - jj
                damp = jnp.where(off >= 0, jnp.exp(-rate * jnp.maximum(off, 0.0)), 0.0) * scale
                sc = lax.dot_general(qh[b * blk:(b + 1) * blk], kh, nt, preferred_element_type=f32)
                wts[h, rows, :] = (sc * damp).astype(jnp.bfloat16)
                gs = lax.dot_general(dh[b * blk:(b + 1) * blk], vh, nt, preferred_element_type=f32)
                gwts[h, rows, :] = (gs * damp).astype(jnp.bfloat16)
        return run

    def intra_task(h, o):
        def run():
            for b in range(nblk):
                rows = pl.ds(b * blk, blk)
                if o == 0:
                    res = jnp.dot(wts[h, rows, :], v_ref[:, cols(h)], preferred_element_type=f32)
                elif o == 1:
                    res = jnp.dot(gwts[h, rows, :], k_ref[:, cols(h)], preferred_element_type=f32)
                elif o == 2:
                    res = lax.dot_general(gwts[h, :, rows], q_ref[:, cols(h)], tn, preferred_element_type=f32)
                else:
                    res = lax.dot_general(wts[h, :, rows], do_ref[:, cols(h)], tn, preferred_element_type=f32)
                intra[o, rows, cols(h)] = res
        return run

    def copy(src, dst, h, slot, other):
        return pltpu.make_async_remote_copy(
            src_ref=src, dst_ref=dst, send_sem=scan_sems.at[0, h, slot], recv_sem=scan_sems.at[1, h, slot],
            device_id=(lax.rem(other + n, n), me), device_id_type=MESH,
        )

    order = []
    for j in range(1, ne):
        for cand in (j, ne - j):
            if 0 < cand < ne and cand not in order:
                order.append(cand)

    def send(o, h):
        for j in order:
            peer = lax.rem(me + j, ne)
            pltpu.make_async_remote_copy(
                src_ref=stage.at[o, pl.ds(pl.multiple_of(peer * slab, slab), slab), cols(h)],
                dst_ref=outs[o].at[:, pl.ds(pl.multiple_of(me * width + h * hd, hd), hd)],
                send_sem=send_sems.at[o, h, j], recv_sem=recv_sems.at[o, h, j],
                device_id=(me_s, peer), device_id_type=MESH,
            ).start()
        pltpu.make_async_copy(
            stage.at[o, pl.ds(pl.multiple_of(me * slab, slab), slab), cols(h)],
            outs[o].at[:, pl.ds(pl.multiple_of(me * width + h * hd, hd), hd)],
            local_sems.at[o, h],
        ).start()

    def pos(b):
        return (lax.broadcasted_iota(jnp.int32, (blk, 1), 0) + b * blk).astype(f32)

    nround = len(near) + 1
    sent = []
    last = len(near)
    pending = []

    def flush_one():
        if pending:
            pending.pop(0)()

    for h in range(heads):
        mine = [weights_task(h)] + [intra_task(h, o) for o in range(4)]
        if h == 0:
            mine = [state_task(g) for g in range(1, heads)] + mine
        per_round = -(-len(mine) // nround)
        kcur, qcur = dk_ref.at[h], dq_ref.at[h]
        for r, d in enumerate(near):
            kc = copy(kcur, krecv.at[r, h], h, 2 * r, me_s + d)
            qc = copy(qcur, qrecv.at[r, h], h, 2 * r + 1, me_s - d)
            pl.when(me_s + d < n)(kc.start)
            pl.when(me_s - d >= 0)(qc.start)
            sent.append((kc, me_s + d < n))
            sent.append((qc, me_s - d >= 0))
            flush_one()
            for task in mine[r * per_round:(r + 1) * per_round]:
                task()
            for cur, nxt, recv, cp, has in ((kcur, kx, krecv, kc, me_s - d >= 0), (qcur, qx, qrecv, qc, me_s + d < n)):
                @pl.when(has)
                def _():
                    cp.wait_recv()
                    nxt[r, h] = cur[...] + wv[r][h] * recv[r, h]

                @pl.when(jnp.logical_not(has))
                def _():
                    nxt[r, h] = cur[...]
            kcur, qcur = kx.at[r, h], qx.at[r, h]
        finals = []
        for j, d in enumerate((1, far)):
            slot = 2 * (last + j)
            kc = copy(kcur, krecv.at[last + j, h], h, slot, me_s + d)
            qc = copy(qcur, qrecv.at[last + j, h], h, slot + 1, me_s - d)
            pl.when(me_s + d < n)(kc.start)
            pl.when(me_s - d >= 0)(qc.start)
            sent.append((kc, me_s + d < n))
            sent.append((qc, me_s - d >= 0))
            finals.append((kc, qc, d))
        flush_one()
        for task in mine[last * per_round:]:
            task()
        s_acc[h] = jnp.zeros((hd, hd), f32)
        r_acc[h] = jnp.zeros((hd, hd), f32)
        for j, (kc, qc, d) in enumerate(finals):
            for cp, recv, acc, has in ((kc, krecv, s_acc, me_s - d >= 0), (qc, qrecv, r_acc, me_s + d < n)):
                @pl.when(has)
                def _():
                    cp.wait_recv()
                    scale = 1.0 if j == 0 else wv[last][h]
                    acc[h] = acc[h] + scale * recv[last + j, h]

        def stage_send(h, o):
            def run():
                rate = rates[h]
                scale = scales[h]
                for b in range(nblk):
                    rows = pl.ds(b * blk, blk)
                    if o == 0:
                        lead = scale * jnp.exp(-rate * pos(b))
                        extra = lead * jnp.dot(q_ref[rows, cols(h)].astype(f32), s_acc[h], precision=hi, preferred_element_type=f32)
                    elif o == 1:
                        lead = scale * jnp.exp(-rate * pos(b))
                        extra = lead * lax.dot_general(do_ref[rows, cols(h)].astype(f32), s_acc[h], nt, precision=hi, preferred_element_type=f32)
                    elif o == 2:
                        trail = scale * jnp.exp(-rate * (length - 1.0 - pos(b)))
                        extra = trail * lax.dot_general(v_ref[rows, cols(h)].astype(f32), r_acc[h], nt, precision=hi, preferred_element_type=f32)
                    else:
                        trail = scale * jnp.exp(-rate * (length - 1.0 - pos(b)))
                        extra = trail * jnp.dot(k_ref[rows, cols(h)].astype(f32), r_acc[h], precision=hi, preferred_element_type=f32)
                    stage[o, rows, cols(h)] = (intra[o, rows, cols(h)] + extra).astype(jnp.bfloat16)
                send(o, h)
            return run

        batches = [stage_send(h, o) for o in range(4)]
        if h < heads - 1:
            batches[0]()
            pending.extend(batches[1:])
        else:
            while pending:
                flush_one()
            for run in batches:
                run()

    for cp, cond in sent:
        pl.when(cond)(cp.wait_send)
    for o in range(4):
        for h in range(heads):
            for j in range(1, ne):
                cp = pltpu.make_async_remote_copy(
                    src_ref=stage.at[o, pl.ds(0, slab), cols(h)],
                    dst_ref=outs[o].at[:, pl.ds(h * hd, hd)],
                    send_sem=send_sems.at[o, h, j], recv_sem=recv_sems.at[o, h, j],
                    device_id=(me_s, lax.rem(me + j, ne)), device_id_type=MESH,
                )
                cp.wait_send()
                cp.wait_recv()
            pltpu.make_async_copy(
                stage.at[o, pl.ds(0, slab), cols(h)], outs[o].at[:, pl.ds(h * hd, hd)], local_sems.at[o, h]
            ).wait()


def settle_kernel(a, b, c, d, oa, ob, oc, od):
    for src, dst in ((a, oa), (b, ob), (c, oc), (d, od)):
        dst[...] = src[...]


def shards(query_tok, key_tok, value_tok, grad_out, decay_rate):
    seg_len = query_tok.shape[0]
    num_heads = decay_rate.shape[0]
    head_size = query_tok.shape[1] // num_heads
    ne = lax.axis_size("exp")
    total_len = seg_len * lax.axis_size("seq")
    n = lax.axis_size("seq")
    near = []
    d = 1
    while 2 * d < n:
        near.append(d)
        d *= 2
    far = d + 1
    nrecv = len(near) + 2
    width = query_tok.shape[1]
    slab = seg_len // ne
    out = jax.ShapeDtypeStruct((slab, ne * width), jnp.bfloat16)
    smem = pl.BlockSpec(memory_space=pltpu.SMEM)
    vspec = pl.BlockSpec(memory_space=pltpu.VMEM)
    anyspec = pl.BlockSpec(memory_space=pl.ANY)
    st = (num_heads, head_size, head_size)
    moved = pl.pallas_call(
        functools.partial(whole_kernel, n, near, far, d, total_len),
        out_shape=(out, out, out, out),
        in_specs=[smem] + [vspec] * 4,
        out_specs=(anyspec, anyspec, anyspec, anyspec),
        scratch_shapes=[
            pltpu.VMEM(st, jnp.float32),
            pltpu.VMEM(st, jnp.float32),
            pltpu.VMEM((len(near),) + st, jnp.float32),
            pltpu.VMEM((len(near),) + st, jnp.float32),
            pltpu.VMEM((nrecv,) + st, jnp.float32),
            pltpu.VMEM((nrecv,) + st, jnp.float32),
            pltpu.VMEM(st, jnp.float32),
            pltpu.VMEM(st, jnp.float32),
            pltpu.VMEM((4, seg_len, width), jnp.float32),
            pltpu.VMEM((4, seg_len, width), jnp.bfloat16),
            pltpu.VMEM((num_heads, seg_len, seg_len), jnp.bfloat16),
            pltpu.VMEM((num_heads, seg_len, seg_len), jnp.bfloat16),
            pltpu.SemaphoreType.DMA((2, num_heads, 2 * nrecv)),
            pltpu.SemaphoreType.DMA((4, num_heads, ne)),
            pltpu.SemaphoreType.DMA((4, num_heads, ne)),
            pltpu.SemaphoreType.DMA((4, num_heads)),
        ],
        compiler_params=pltpu.CompilerParams(
            collective_id=0, has_side_effects=True, vmem_limit_bytes=56 * 1024 * 1024
        ),
    )(decay_rate.astype(jnp.float32), query_tok, key_tok, value_tok, grad_out)
    return pl.pallas_call(
        settle_kernel,
        out_shape=(out, out, out, out),
        in_specs=[vspec] * 4,
        out_specs=(vspec, vspec, vspec, vspec),
    )(*moved)


def solution(mesh):
    placed = (P("seq", "exp"), P("seq", "exp"), P("seq", "exp"), P("seq", "exp"), P("exp"))
    return jax.shard_map(
        shards,
        mesh=mesh,
        in_specs=placed,
        out_specs=(
            P(("seq", "exp"), None),
            P(("seq", "exp"), None),
            P(("seq", "exp"), None),
            P(("seq", "exp"), None),
        ),
        check_vma=False,
    )
```
